32 devices in a mesh: energy: 2 (over x), chain: 16 (over z, y, core).
Axes of the slice: x: 2, y: 2, z: 4, core: 2. Of those that a mesh axis runs over, the one named last changes fastest.
Arguments:
- lower: bfloat16 [32, 2, 256, 256], P(('energy', 'chain')), parts along dimension 0, may hold values from -0.125 to 0.125
- upper: bfloat16 [32, 2, 256, 256], P(('energy', 'chain')), parts along dimension 0, may hold values from -0.125 to 0.125
- right_side: bfloat16 [32, 2, 256, 256], P(('energy', 'chain')), parts along dimension 0, may hold values from -6 to 6
Outputs:
- reduced_rhs: bfloat16 [32, 2, 256, 256], P(('energy', 'chain')), parts along dimension 0
The draws below stay inside these ranges and needn't reach their ends.
There are 2 independent parts, one for each index of `energy`. The reference program is written for one: setup_inputs(seed, part) draws one part's arguments, and reference() takes and returns one part's arrays. A program takes and returns all parts, laid end to end along the dimension named above; each array names one. Nothing has to cross between parts.
All inputs are finite; a program needn't handle non-finite values.
Results may differ from the reference program's by a relative error of at most 0.011.
Values may be sent and summed in bfloat16 or wider, within the bound.
A program may use at most 64 MiB of HBM per device.

```python
import jax
import jax.numpy as jnp

M = 256
COLS = 256
SECTIONS = 3
NS_STEPS = 2
ROWS = 16


def block_scale(stream_key, shape, shards, least, high):
    def one(axis_at, parts):
        steps = jax.random.uniform(jax.random.fold_in(jax.random.fold_in(stream_key, 6), axis_at), (parts,), jnp.float32, least / len(shards), high / len(shards))
        return jnp.repeat(jnp.exp(steps), shape[axis_at] // parts).reshape((-1,) + (1,) * (len(shape) - axis_at - 1))

    loudness = one(*shards[0])
    for cut in shards[1:]:
        loudness = loudness * one(*cut)
    return loudness


def scatter_about(key, extent, spread, most, split=(), kind=jnp.bfloat16):
    level = block_scale(key, extent, split, -0.22, 0.18) if split else 1.0
    entries = jax.random.normal(key, extent, jnp.float32) * spread * level
    return jnp.minimum(jnp.maximum(entries, -most), most).astype(kind)


def setup_inputs(seed: int = 0, part: int = 0) -> dict:
    arg_keys = jax.random.split(jax.random.key(seed), 4)
    part_keys = jax.random.split(jax.random.fold_in(arg_keys[3], part), 4)
    return {
        "lower": scatter_about(part_keys[0], (ROWS, 2, M, M), (7 * M) ** -0.5, 0.125, ((0, 16),)),
        "upper": scatter_about(part_keys[1], (ROWS, 2, M, M), (7 * M) ** -0.5, 0.125, ((0, 16),)),
        "right_side": scatter_about(part_keys[2], (ROWS, 2, M, COLS), 1.0, 6.0, ((0, 16),)),
    }


def complex_product(left_block, right_block):
    left_f = left_block.astype(jnp.float32)
    right_f = right_block.astype(jnp.float32)
    real_part = jnp.einsum("nij,njk->nik", left_f[:, 0], right_f[:, 0]) - jnp.einsum("nij,njk->nik", left_f[:, 1], right_f[:, 1])
    imag_part = jnp.einsum("nij,njk->nik", left_f[:, 0], right_f[:, 1]) + jnp.einsum("nij,njk->nik", left_f[:, 1], right_f[:, 0])
    return jnp.stack([real_part, imag_part], axis=1)


def from_below(values, reach):
    padding = jnp.zeros_like(values[:reach])
    return jnp.concatenate([padding, values[:-reach]], axis=0)


def from_above(values, reach):
    padding = jnp.zeros_like(values[:reach])
    return jnp.concatenate([values[reach:], padding], axis=0)


def approx_inverse(diagonal_new, identity_block):
    diagonal_low = diagonal_new.astype(jnp.bfloat16)
    approx = (2.0 * identity_block - diagonal_new).astype(jnp.bfloat16)
    for repeat in range(NS_STEPS):
        correction = (2.0 * identity_block - complex_product(diagonal_low, approx)).astype(jnp.bfloat16)
        approx = complex_product(approx, correction).astype(jnp.bfloat16)
    return approx


def reference(lower, upper, right_side):
    unit_matrix = jnp.eye(M, dtype=jnp.float32)
    identity_block = jnp.stack([unit_matrix, jnp.zeros_like(unit_matrix)])[None]
    lower_block = lower
    upper_block = upper
    current = right_side
    for number in range(SECTIONS):
        reach = 2 ** number
        final = number == SECTIONS - 1
        below_lower = from_below(lower_block, reach)
        below_upper = from_below(upper_block, reach)
        below_rhs = from_below(current, reach)
        above_lower = from_above(lower_block, reach)
        above_upper = from_above(upper_block, reach)
        above_rhs = from_above(current, reach)
        diagonal_new = identity_block - complex_product(lower_block, below_upper) - complex_product(upper_block, above_lower)
        inverse = approx_inverse(diagonal_new, identity_block)
        rhs_new = (current - complex_product(lower_block, below_rhs) - complex_product(upper_block, above_rhs)).astype(jnp.bfloat16)
        if not final:
            lower_raw = (-complex_product(lower_block, below_lower)).astype(jnp.bfloat16)
            upper_raw = (-complex_product(upper_block, above_upper)).astype(jnp.bfloat16)
            lower_block = complex_product(inverse, lower_raw).astype(jnp.bfloat16)
            upper_block = complex_product(inverse, upper_raw).astype(jnp.bfloat16)
        current = complex_product(inverse, rhs_new).astype(jnp.bfloat16)
    return current
```

```python
import functools

import jax
import jax.numpy as jnp
from jax import lax
from jax.experimental import pallas as pl
from jax.experimental.pallas import tpu as pltpu
from jax.sharding import PartitionSpec as P

NS_STEPS = 2
MESH = pl.DeviceIdType.MESH
LOW = jnp.bfloat16

F, K = 0, 1
OWN, FW, BW = 0, 1, 2


def dot(left, right):
    return jnp.dot(left, right, preferred_element_type=jnp.float32)


def product(*pairs):
    left = jnp.concatenate([part for l, _ in pairs for part in (l[0], l[1])], axis=1)
    real = jnp.concatenate([part for _, r in pairs for part in (r[0], -r[1])], axis=0)
    imag = jnp.concatenate([part for _, r in pairs for part in (r[1], r[0])], axis=0)
    return dot(left, real), dot(left, imag)


def rhs_product(*pairs):
    left = jnp.concatenate([part for l, _ in pairs for part in (l[0], l[1])], axis=1)
    right = []
    for _, r in pairs:
        wide = r.shape[1] // 2
        right += [r, jnp.concatenate([-r[:, wide:], r[:, :wide]], axis=1)]
    return dot(left, jnp.concatenate(right, axis=0))


def rounded(parts):
    return jnp.stack([parts[0].astype(LOW), parts[1].astype(LOW)])


def negated(parts):
    return -parts[0], -parts[1]


def kernel(
    quads, l_ref, u_ref, b_ref, out_ref,
    u0, b0, own1, bown1, u1, b1, own2, bown2, u2, b2, last, inv, raw, low, fix,
    sem_load, sem_bload, sem_m, sem_y, sem_d, sem_r,
    sem_1m, sem_1z, sem_1r, sem_2s, sem_2r, sem_out,
):
    me = lax.axis_index("chain")
    q = me // 4
    a = (me // 2) % 2
    b = me % 2
    inner = a != b
    outer = a == b
    qf, qb = q + 1 - 2 * a, q - 1 + 2 * a
    has_fw = (qf >= 0) & (qf < quads)
    has_bw = (qb >= 0) & (qb < quads)
    order = l_ref.shape[2]
    wide = b_ref.shape[3] // 2

    def at(quad, y, core):
        return {"chain": quad * 4 + y * 2 + core}

    mate = at(q, a, 1 - b)
    across = at(q, 1 - a, b)
    twin = at(q, b, a)
    fw, bw = at(qf, a, b), at(qb, a, b)
    side = {"chain": jnp.where(inner, at(qf, a, 1 - b)["chain"], at(qb, a, 1 - b)["chain"])}
    has_side = (inner & has_fw) | (outer & has_bw)
    diag = at(qb, 1 - a, 1 - b)
    has_diag = outer & has_bw

    def local(src, dst, sem):
        return pltpu.make_async_copy(src, dst, sem)

    def remote(src, dst, send, recv, who):
        return pltpu.make_async_remote_copy(
            src_ref=src, dst_ref=dst, send_sem=send, recv_sem=recv,
            device_id=who, device_id_type=MESH,
        )

    def arrive(ref, sem):
        pltpu.make_async_copy(ref, ref, sem).wait()

    def when(condition, action):
        pl.when(condition)(action)

    home = jnp.where(outer, OWN, BW)

    def load(unit):
        place = jnp.where(a == 0, 1 - unit, unit)
        return local((l_ref, u_ref)[unit].at[0], u0.at[home, place], sem_load.at[unit])

    def load_rhs(half, part):
        return local(
            b_ref.at[0, part, :, pl.ds(half * wide, wide)],
            b0.at[home, half, :, pl.ds(part * wide, wide)],
            sem_bload.at[half, part],
        )

    for unit in range(2):
        load(unit).start()
    for half in range(2):
        for part in range(2):
            load_rhs(half, part).start()

    barrier = pltpu.get_barrier_semaphore()

    def greet(who):
        pl.semaphore_signal(barrier, inc=1, device_id=who, device_id_type=MESH)

    greet(mate)
    greet(across)
    greetings = ((has_side, side), (has_diag, diag), (inner, twin), (has_fw, fw), (has_bw, bw))
    count = 2
    for exists, who in greetings:
        when(exists, functools.partial(greet, who))
        count = count + exists.astype(jnp.int32)

    def clear(ref):
        ref[...] = jnp.zeros(ref.shape, ref.dtype)

    has_one = {FW: outer | has_fw, BW: inner | has_bw}
    has_two = {FW: has_fw, BW: has_bw}

    @pl.when(outer & jnp.logical_not(has_bw))
    def _():
        clear(u0.at[BW])
        clear(b0.at[BW])

    for slot in (FW, BW):
        @pl.when(jnp.logical_not(has_one[slot]))
        def _():
            clear(u1.at[slot - 1])
            clear(b1.at[slot - 1])

        @pl.when(jnp.logical_not(has_two[slot]))
        def _():
            clear(u2.at[slot - 1])
            clear(b2.at[slot - 1])

    for unit in range(2):
        load(unit).wait()
    pl.semaphore_wait(barrier, count)

    def to_mate(item):
        if item < 2:
            src, dst = u0.at[BW, item], u0.at[FW, item]
        else:
            src, dst = b0.at[BW, item - 2], b0.at[FW, item - 2]
        return remote(src, dst, sem_m.at[0, item], sem_m.at[1, item], mate)

    def mate_in(item):
        ref = u0.at[FW, item] if item < 2 else b0.at[FW, item - 2]
        arrive(ref, sem_m.at[1, item])

    def y_place(item):
        if item < 8:
            return u0.at[FW if item < 4 else OWN, (item // 2) % 2, item % 2]
        return b0.at[FW if item < 10 else OWN, item % 2]

    def over_y(item):
        if item < 8:
            src = u0.at[OWN if item < 4 else FW, 1 - (item // 2) % 2, item % 2]
        else:
            src = b0.at[OWN if item < 10 else FW, item % 2]
        return remote(src, y_place(item), sem_y.at[0, item], sem_y.at[1, item], across)

    def y_in(item):
        arrive(y_place(item), sem_y.at[1, item])

    def relay(item):
        return remote(
            y_place(item), u0.at[BW, item // 2, item % 2],
            sem_r.at[0, item], sem_r.at[1, item], side,
        )

    def relay_in(item):
        arrive(u0.at[BW, item // 2, item % 2], sem_r.at[1, item])

    def over_diag(half):
        return remote(
            b0.at[OWN, half], b0.at[BW, half], sem_d.at[0, half], sem_d.at[1, half], diag
        )

    def wait_rhs():
        for half in range(2):
            for part in range(2):
                load_rhs(half, part).wait()

    @pl.when(inner)
    def _():
        to_mate(K).start()
        to_mate(F).start()
        wait_rhs()
        for half in range(2):
            to_mate(2 + half).start()
        for item in range(4):
            y_in(item)
            when(has_fw, lambda item=item: relay(item).start())
        for item in (4, 5):
            y_in(item)

    @pl.when(outer)
    def _():
        for item in range(4):
            over_y(item).start()
        mate_in(K)
        for item in (4, 5):
            over_y(item).start()
        mate_in(F)
        for item in (6, 7):
            over_y(item).start()
        wait_rhs()
        for item in (8, 9):
            over_y(item).start()
        for half in range(2):
            mate_in(2 + half)
        for item in (10, 11):
            over_y(item).start()

    row = lax.broadcasted_iota(jnp.int32, (order, order), 0)
    col = lax.broadcasted_iota(jnp.int32, (order, order), 1)
    unit_matrix = (row == col).astype(jnp.float32)

    def inverse(off, number):
        x = inv.at[number]
        low[...] = rounded((unit_matrix - off[0], -off[1]))
        x[...] = rounded((unit_matrix + off[0], off[1]))
        for _ in range(NS_STEPS):
            prod = product((low[...], x[...]))
            fix[...] = rounded((2.0 * unit_matrix - prod[0], -prod[1]))
            x[...] = rounded(product((x[...], fix[...])))

    def new_rhs(number, own, k, f, behind, ahead):
        change = rhs_product((k, behind), (f, ahead))
        residual = (own.astype(jnp.float32) - change).astype(LOW)
        return rhs_product((inv[number], residual)).astype(LOW)

    mate_slot = jnp.where(outer, BW - 1, FW - 1)
    side_slot = jnp.where(outer, FW - 1, BW - 1)

    def send1(item, slot, sem, who):
        if item < 2:
            src, dst = own1.at[item], u1.at[slot, item]
        else:
            src, dst = bown1.at[item - 2], b1.at[slot, item - 2]
        return remote(src, dst, sem.at[item], sem_1r.at[slot, item], who)

    def to_side1(item):
        return send1(item, side_slot, sem_1z, side)

    def to_mate1(item):
        return send1(item, mate_slot, sem_1m, mate)

    def start1(item):
        when(has_side, lambda: to_side1(item).start())
        to_mate1(item).start()

    def in1(slot, item):
        ref = u1.at[slot - 1, item] if item < 2 else b1.at[slot - 1, item - 2]
        when(has_one[slot], lambda: arrive(ref, sem_1r.at[slot - 1, item]))

    def send2(item, ahead):
        slot = (BW if ahead else FW) - 1
        if item == 0:
            src, dst = own2.at[F if ahead else K], u2.at[slot]
        else:
            src, dst = bown2.at[item - 1], b2.at[slot, item - 1]
        way = 0 if ahead else 1
        return remote(
            src, dst, sem_2s.at[way, item], sem_2r.at[slot, item], fw if ahead else bw
        )

    def start2(item, ahead):
        when(has_fw if ahead else has_bw, lambda: send2(item, ahead).start())

    def in2(slot, item):
        ref = u2.at[slot - 1] if item == 0 else b2.at[slot - 1, item - 1]
        when(has_two[slot], lambda: arrive(ref, sem_2r.at[slot - 1, item]))

    raw[F] = rounded(negated(product((u0[OWN, F], u0[FW, F]))))

    @pl.when(inner)
    def _():
        for item in (6, 7):
            y_in(item)

    @pl.when(has_diag)
    def _():
        for item in (0, 1):
            relay_in(item)

    inverse(product((u0[OWN, K], u0[BW, F]), (u0[OWN, F], u0[FW, K])), 0)
    own1[F] = rounded(product((inv[0], raw[F])))
    start1(F)

    @pl.when(has_diag)
    def _():
        for item in (2, 3):
            relay_in(item)

    raw[K] = rounded(negated(product((u0[OWN, K], u0[BW, K]))))
    own1[K] = rounded(product((inv[0], raw[K])))
    start1(K)

    def rhs0():
        for half in range(2):
            @pl.when(inner)
            def _():
                y_in(8 + half)
                y_in(10 + half)

            when(has_diag, lambda: arrive(b0.at[BW, half], sem_d.at[1, half]))
            bown1[half] = new_rhs(
                0, b0[OWN, half], u0[OWN, K], u0[OWN, F], b0[BW, half], b0[FW, half]
            )
            start1(2 + half)

    @pl.when(outer)
    def _():
        for item in (6, 7):
            over_y(item).wait_send()
        for half in range(2):
            when(has_bw, lambda half=half: over_diag(half).start())
        rhs0()

    in1(FW, K)
    in1(BW, F)
    inverse(product((own1[K], u1[BW - 1, F]), (own1[F], u1[FW - 1, K])), 1)

    def factor1(unit):
        slot = FW if unit == F else BW
        in1(slot, unit)
        raw[unit] = rounded(negated(product((own1[unit], u1[slot - 1, unit]))))
        own2[unit] = rounded(product((inv[1], raw[unit])))
        start2(0, unit == F)

    @pl.when(outer)
    def _():
        factor1(F)
        factor1(K)

    @pl.when(inner)
    def _():
        factor1(K)
        factor1(F)
        rhs0()

    for half in range(2):
        in1(FW, 2 + half)
        in1(BW, 2 + half)
        bown2[half] = new_rhs(
            1, bown1[half], own1[K], own1[F], b1[BW - 1, half], b1[FW - 1, half]
        )
        start2(1 + half, True)
        start2(1 + half, False)

    def spot(half, part):
        return (
            last.at[half, :, pl.ds(part * wide, wide)],
            out_ref.at[0, part, :, pl.ds(half * wide, wide)],
        )

    def give(half, part):
        src, dst = spot(half, part)
        return remote(src, dst, sem_out.at[0, half, part], sem_out.at[1, half, part], twin)

    def keep(half, part):
        src, dst = spot(half, part)
        return local(src, dst, sem_out.at[1, half, part])

    in2(FW, 0)
    in2(BW, 0)
    inverse(product((own2[K], u2[BW - 1]), (own2[F], u2[FW - 1])), 2)
    for half in range(2):
        in2(FW, 1 + half)
        in2(BW, 1 + half)
        last[half] = new_rhs(
            2, bown2[half], own2[K], own2[F], b2[BW - 1, half], b2[FW - 1, half]
        )
        for part in range(2):
            when(inner, lambda half=half, part=part: give(half, part).start())
            when(outer, lambda half=half, part=part: keep(half, part).start())

    @pl.when(inner)
    def _():
        for item in range(4):
            to_mate(item).wait_send()
            when(has_fw, lambda item=item: relay(item).wait_send())

    @pl.when(outer)
    def _():
        for item in range(12):
            if item not in (6, 7):
                over_y(item).wait_send()
        for half in range(2):
            when(has_bw, lambda half=half: over_diag(half).wait_send())

    for item in range(4):
        when(has_side, lambda item=item: to_side1(item).wait_send())
        to_mate1(item).wait_send()
    for item in range(3):
        when(has_fw, lambda item=item: send2(item, True).wait_send())
        when(has_bw, lambda item=item: send2(item, False).wait_send())
    for half in range(2):
        for part in range(2):
            when(inner, lambda half=half, part=part: give(half, part).wait())
            when(outer, lambda half=half, part=part: keep(half, part).wait())


def local_call(quads, lower, upper, right_side):
    block = lower.shape[1:]
    half = (right_side.shape[2], right_side.shape[3])
    anywhere = pl.BlockSpec(memory_space=pl.ANY)
    dma = pltpu.SemaphoreType.DMA
    vmem = lambda *shape: pltpu.VMEM(shape, LOW)
    return pl.pallas_call(
        functools.partial(kernel, quads),
        out_shape=jax.ShapeDtypeStruct(right_side.shape, right_side.dtype),
        in_specs=[anywhere] * 3,
        out_specs=anywhere,
        scratch_shapes=[
            vmem(3, 2, *block),
            vmem(3, 2, *half),
            vmem(2, *block),
            vmem(2, *half),
            vmem(2, 2, *block),
            vmem(2, 2, *half),
            vmem(2, *block),
            vmem(2, *half),
            vmem(2, *block),
            vmem(2, 2, *half),
            vmem(2, *half),
            vmem(3, *block),
            vmem(2, *block),
            vmem(*block),
            vmem(*block),
            dma((2,)),
            dma((2, 2)),
            dma((2, 4)),
            dma((2, 12)),
            dma((2, 2)),
            dma((2, 4)),
            dma((4,)),
            dma((4,)),
            dma((2, 4)),
            dma((2, 3)),
            dma((2, 3)),
            dma((2, 2, 2)),
        ],
        compiler_params=pltpu.CompilerParams(collective_id=0, has_side_effects=True),
    )(lower, upper, right_side)


def solution(mesh):
    placed = P(("energy", "chain"), None, None, None)
    return jax.shard_map(
        functools.partial(local_call, mesh.shape["chain"] // 4),
        mesh=mesh,
        in_specs=(placed,) * 3,
        out_specs=placed,
        check_vma=False,
    )
```

```python
import functools

import jax
import jax.numpy as jnp
from jax import lax
from jax.experimental import pallas as pl
from jax.experimental.pallas import tpu as pltpu
from jax.sharding import PartitionSpec as P

NS_STEPS = 2
MESH = pl.DeviceIdType.MESH
LOW = jnp.bfloat16

F, K = 0, 1
OWN, FW, BW = 0, 1, 2
SOWN, SFAR = 3, 4


def dot(left, right):
    return jnp.dot(left, right, preferred_element_type=jnp.float32)


def product(*pairs):
    left = jnp.concatenate([part for l, _ in pairs for part in (l[0], l[1])], axis=1)
    real = jnp.concatenate([part for _, r in pairs for part in (r[0], -r[1])], axis=0)
    imag = jnp.concatenate([part for _, r in pairs for part in (r[1], r[0])], axis=0)
    return dot(left, real), dot(left, imag)


def rhs_product(*pairs):
    left = jnp.concatenate([part for l, _ in pairs for part in (l[0], l[1])], axis=1)
    right = []
    for _, r in pairs:
        wide = r.shape[1] // 2
        right += [r, jnp.concatenate([-r[:, wide:], r[:, :wide]], axis=1)]
    return dot(left, jnp.concatenate(right, axis=0))


def rounded(parts):
    return jnp.stack([parts[0].astype(LOW), parts[1].astype(LOW)])


def negated(parts):
    return -parts[0], -parts[1]


def kernel(
    quads, l_ref, u_ref, b_ref, out_ref,
    u0, b0, own1, bown1, u1, b1, own2, bown2, u2, b2, last, inv, raw, side_raw, low, fix,
    sem_load, sem_bload, sem_m, sem_y, sem_d, sem_s,
    sem_1m, sem_1z, sem_1r, sem_2s, sem_2r, sem_out,
):
    me = lax.axis_index("chain")
    q = me // 4
    a = (me // 2) % 2
    b = me % 2
    inner = a != b
    outer = a == b
    qf, qb = q + 1 - 2 * a, q - 1 + 2 * a
    has_fw = (qf >= 0) & (qf < quads)
    has_bw = (qb >= 0) & (qb < quads)
    order = l_ref.shape[2]
    wide = b_ref.shape[3] // 2

    def at(quad, y, core):
        return {"chain": quad * 4 + y * 2 + core}

    mate = at(q, a, 1 - b)
    across = at(q, 1 - a, b)
    twin = at(q, b, a)
    fw, bw = at(qf, a, b), at(qb, a, b)
    side = {"chain": jnp.where(inner, at(qf, a, 1 - b)["chain"], at(qb, a, 1 - b)["chain"])}
    has_side = (inner & has_fw) | (outer & has_bw)
    diag = at(qb, 1 - a, 1 - b)
    has_diag = outer & has_bw

    def local(src, dst, sem):
        return pltpu.make_async_copy(src, dst, sem)

    def remote(src, dst, send, recv, who):
        return pltpu.make_async_remote_copy(
            src_ref=src, dst_ref=dst, send_sem=send, recv_sem=recv,
            device_id=who, device_id_type=MESH,
        )

    def arrive(ref, sem):
        pltpu.make_async_copy(ref, ref, sem).wait()

    def when(condition, action):
        pl.when(condition)(action)

    home = jnp.where(outer, OWN, BW)

    def load(unit):
        place = jnp.where(a == 0, 1 - unit, unit)
        return local((l_ref, u_ref)[unit].at[0], u0.at[home, place], sem_load.at[unit])

    def load_rhs(half, part):
        return local(
            b_ref.at[0, part, :, pl.ds(half * wide, wide)],
            b0.at[home, half, :, pl.ds(part * wide, wide)],
            sem_bload.at[half, part],
        )

    for unit in range(2):
        load(unit).start()
    for half in range(2):
        for part in range(2):
            load_rhs(half, part).start()

    barrier = pltpu.get_barrier_semaphore()

    def greet(who):
        pl.semaphore_signal(barrier, inc=1, device_id=who, device_id_type=MESH)

    greet(mate)
    greet(across)
    greetings = ((has_side, side), (has_diag, diag), (inner, twin), (has_fw, fw), (has_bw, bw))
    count = 2
    for exists, who in greetings:
        when(exists, functools.partial(greet, who))
        count = count + exists.astype(jnp.int32)

    def clear(ref):
        ref[...] = jnp.zeros(ref.shape, ref.dtype)

    has_one = {FW: outer | has_fw, BW: inner | has_bw}
    has_two = {FW: has_fw, BW: has_bw}

    @pl.when(outer & jnp.logical_not(has_bw))
    def _():
        clear(u0.at[BW])
        clear(b0.at[BW])

    @pl.when(jnp.logical_not(has_side))
    def _():
        clear(u0.at[SOWN])
        clear(u0.at[SFAR])

    for slot in (FW, BW):
        @pl.when(jnp.logical_not(has_one[slot]))
        def _():
            clear(b1.at[slot - 1])

        @pl.when(jnp.logical_not(has_two[slot]))
        def _():
            clear(u2.at[slot - 1])
            clear(b2.at[slot - 1])

    for unit in range(2):
        load(unit).wait()
    pl.semaphore_wait(barrier, count)

    def to_mate(item):
        if item < 2:
            src, dst = u0.at[BW, item], u0.at[FW, item]
        else:
            src, dst = b0.at[BW, item - 2], b0.at[FW, item - 2]
        return remote(src, dst, sem_m.at[0, item], sem_m.at[1, item], mate)

    def mate_in(item):
        ref = u0.at[FW, item] if item < 2 else b0.at[FW, item - 2]
        arrive(ref, sem_m.at[1, item])

    def y_place(item):
        if item < 8:
            return u0.at[FW if item < 4 else OWN, (item // 2) % 2, item % 2]
        return b0.at[FW if item < 10 else OWN, item % 2]

    def over_y(item):
        if item < 8:
            src = u0.at[OWN if item < 4 else FW, 1 - (item // 2) % 2, item % 2]
        else:
            src = b0.at[OWN if item < 10 else FW, item % 2]
        return remote(src, y_place(item), sem_y.at[0, item], sem_y.at[1, item], across)

    def y_in(item):
        arrive(y_place(item), sem_y.at[1, item])

    def to_side(source, place, unit, part):
        return remote(
            u0.at[source, unit, part], u0.at[place, unit, part],
            sem_s.at[0, place - BW, unit, part], sem_s.at[1, place - BW, unit, part], side,
        )

    def start_side(source, place, unit):
        for part in range(2):
            when(has_side, lambda part=part: to_side(source, place, unit, part).start())

    def side_in(place, unit):
        for part in range(2):
            ref, sem = u0.at[place, unit, part], sem_s.at[1, place - BW, unit, part]
            when(has_side, lambda ref=ref, sem=sem: arrive(ref, sem))

    def hand_on(item):
        y_in(item)
        source, place = (FW, BW) if item < 4 else (OWN, SOWN)
        when(has_side, lambda: to_side(source, place, (item // 2) % 2, item % 2).start())

    def over_diag(half):
        return remote(
            b0.at[OWN, half], b0.at[BW, half], sem_d.at[0, half], sem_d.at[1, half], diag
        )

    def wait_rhs():
        for half in range(2):
            for part in range(2):
                load_rhs(half, part).wait()

    row = lax.broadcasted_iota(jnp.int32, (order, order), 0)
    col = lax.broadcasted_iota(jnp.int32, (order, order), 1)
    unit_matrix = (row == col).astype(jnp.float32)

    def inverse(*jobs):
        for place, (off, number) in enumerate(jobs):
            low[place] = rounded((unit_matrix - off[0], -off[1]))
            inv[number] = rounded((unit_matrix + off[0], off[1]))
        for _ in range(NS_STEPS):
            for place, (_, number) in enumerate(jobs):
                prod = product((low[place], inv[number]))
                fix[place] = rounded((2.0 * unit_matrix - prod[0], -prod[1]))
            for place, (_, number) in enumerate(jobs):
                inv[number] = rounded(product((inv[number], fix[place])))

    def crossed(left, right):
        return rounded(negated(product((left, right))))

    def solved(number, right):
        return rounded(product((inv[number], right)))

    def new_rhs(number, own, k, f, behind, ahead):
        change = rhs_product((k, behind), (f, ahead))
        residual = (own.astype(jnp.float32) - change).astype(LOW)
        return rhs_product((inv[number], residual)).astype(LOW)

    mate_slot = jnp.where(outer, BW - 1, FW - 1)
    side_slot = jnp.where(outer, FW - 1, BW - 1)

    def send1(item, slot, sem, who):
        if item < 2:
            src, dst = own1.at[item], u1.at[slot, item]
        else:
            src, dst = bown1.at[item - 2], b1.at[slot, item - 2]
        return remote(src, dst, sem.at[item], sem_1r.at[slot, item], who)

    def to_side1(item):
        return send1(item, side_slot, sem_1z, side)

    def to_mate1(item):
        return send1(item, mate_slot, sem_1m, mate)

    def start1(item):
        if item >= 2:
            when(has_side, lambda: to_side1(item).start())
        to_mate1(item).start()

    def in1(slot, item):
        ref = u1.at[slot - 1, item] if item < 2 else b1.at[slot - 1, item - 2]
        when(has_one[slot], lambda: arrive(ref, sem_1r.at[slot - 1, item]))

    def send2(item, ahead):
        slot = (BW if ahead else FW) - 1
        if item == 0:
            src, dst = own2.at[F if ahead else K], u2.at[slot]
        else:
            src, dst = bown2.at[item - 1], b2.at[slot, item - 1]
        way = 0 if ahead else 1
        return remote(
            src, dst, sem_2s.at[way, item], sem_2r.at[slot, item], fw if ahead else bw
        )

    def start2(item, ahead):
        when(has_fw if ahead else has_bw, lambda: send2(item, ahead).start())

    def in2(slot, item):
        ref = u2.at[slot - 1] if item == 0 else b2.at[slot - 1, item - 1]
        when(has_two[slot], lambda: arrive(ref, sem_2r.at[slot - 1, item]))

    def rhs0():
        for half in range(2):
            @pl.when(inner)
            def _():
                y_in(8 + half)
                y_in(10 + half)

            when(has_diag, lambda: arrive(b0.at[BW, half], sem_d.at[1, half]))
            bown1[half] = new_rhs(
                0, b0[OWN, half], u0[OWN, K], u0[OWN, F], b0[BW, half], b0[FW, half]
            )
            start1(2 + half)

    def inverse1():
        inverse((product((own1[K], u1[BW - 1, F]), (own1[F], u1[FW - 1, K])), 1))

    def factor1(unit):
        slot = FW if unit == F else BW
        raw[unit] = crossed(own1[unit], u1[slot - 1, unit])
        own2[unit] = solved(1, raw[unit])
        start2(0, unit == F)

    @pl.when(inner)
    def _():
        to_mate(K).start()
        to_mate(F).start()
        start_side(BW, SFAR, F)
        wait_rhs()
        for half in range(2):
            to_mate(2 + half).start()
        for item in range(4):
            hand_on(item)
        side_in(SOWN, K)
        side_raw[K] = crossed(u0[SOWN, K], u0[FW, K])
        for item in (4, 5):
            hand_on(item)
        raw[F] = crossed(u0[OWN, F], u0[FW, F])
        side_in(SOWN, F)
        side_in(SFAR, K)
        for item in (6, 7):
            hand_on(item)
        start_side(BW, SFAR, K)
        inverse(
            (product((u0[OWN, K], u0[BW, F]), (u0[OWN, F], u0[FW, K])), 0),
            (product((u0[SOWN, K], u0[FW, F]), (u0[SOWN, F], u0[SFAR, K])), 3),
        )
        raw[K] = crossed(u0[OWN, K], u0[BW, K])
        own1[F] = solved(0, raw[F])
        start1(F)
        own1[K] = solved(0, raw[K])
        start1(K)
        u1[FW - 1, K] = solved(3, side_raw[K])
        side_in(SFAR, F)
        in1(BW, F)
        inverse1()
        side_raw[F] = crossed(u0[SOWN, F], u0[SFAR, F])
        u1[FW - 1, F] = solved(3, side_raw[F])
        factor1(F)
        in1(BW, K)
        factor1(K)
        rhs0()

    @pl.when(outer)
    def _():
        for item in range(4):
            over_y(item).start()
        start_side(OWN, SOWN, K)
        start_side(OWN, SOWN, F)
        mate_in(K)
        for item in (4, 5):
            over_y(item).start()
        start_side(FW, SFAR, K)
        mate_in(F)
        for item in (6, 7):
            over_y(item).start()
        start_side(FW, SFAR, F)
        wait_rhs()
        for item in (8, 9):
            over_y(item).start()
        for half in range(2):
            mate_in(2 + half)
        for item in (10, 11):
            over_y(item).start()
        raw[F] = crossed(u0[OWN, F], u0[FW, F])
        side_in(BW, F)
        inverse((product((u0[OWN, K], u0[BW, F]), (u0[OWN, F], u0[FW, K])), 0))
        own1[F] = solved(0, raw[F])
        start1(F)
        side_in(BW, K)
        raw[K] = crossed(u0[OWN, K], u0[BW, K])
        own1[K] = solved(0, raw[K])
        start1(K)
        for item in (6, 7):
            over_y(item).wait_send()
        for half in range(2):
            when(has_bw, lambda half=half: over_diag(half).start())
        side_in(SOWN, F)
        side_raw[F] = crossed(u0[SOWN, F], u0[BW, F])
        side_in(SFAR, F)
        side_in(SOWN, K)
        inverse((product((u0[SOWN, K], u0[SFAR, F]), (u0[SOWN, F], u0[BW, K])), 3))
        u1[BW - 1, F] = solved(3, side_raw[F])
        in1(FW, F)
        in1(FW, K)
        inverse1()
        factor1(F)
        rhs0()
        side_in(SFAR, K)
        side_raw[K] = crossed(u0[SOWN, K], u0[SFAR, K])
        u1[BW - 1, K] = solved(3, side_raw[K])
        factor1(K)

    for half in range(2):
        in1(FW, 2 + half)
        in1(BW, 2 + half)
        bown2[half] = new_rhs(
            1, bown1[half], own1[K], own1[F], b1[BW - 1, half], b1[FW - 1, half]
        )
        start2(1 + half, True)
        start2(1 + half, False)

    def spot(half, part):
        return (
            last.at[half, :, pl.ds(part * wide, wide)],
            out_ref.at[0, part, :, pl.ds(half * wide, wide)],
        )

    def give(half, part):
        src, dst = spot(half, part)
        return remote(src, dst, sem_out.at[0, half, part], sem_out.at[1, half, part], twin)

    def keep(half, part):
        src, dst = spot(half, part)
        return local(src, dst, sem_out.at[1, half, part])

    in2(FW, 0)
    in2(BW, 0)
    inverse((product((own2[K], u2[BW - 1]), (own2[F], u2[FW - 1])), 2))
    for half in range(2):
        in2(FW, 1 + half)
        in2(BW, 1 + half)
        last[half] = new_rhs(
            2, bown2[half], own2[K], own2[F], b2[BW - 1, half], b2[FW - 1, half]
        )
        for part in range(2):
            when(inner, lambda half=half, part=part: give(half, part).start())
            when(outer, lambda half=half, part=part: keep(half, part).start())

    @pl.when(inner)
    def _():
        for item in range(4):
            to_mate(item).wait_send()

    @pl.when(outer)
    def _():
        for item in range(12):
            if item not in (6, 7):
                over_y(item).wait_send()
        for half in range(2):
            when(has_bw, lambda half=half: over_diag(half).wait_send())

    def side_sent(source, place):
        for unit in range(2):
            for part in range(2):
                to_side(source, place, unit, part).wait_send()

    @pl.when(inner & has_side)
    def _():
        side_sent(FW, BW)
        side_sent(OWN, SOWN)
        side_sent(BW, SFAR)

    @pl.when(outer & has_side)
    def _():
        side_sent(OWN, SOWN)
        side_sent(FW, SFAR)

    for item in range(4):
        if item >= 2:
            when(has_side, lambda item=item: to_side1(item).wait_send())
        to_mate1(item).wait_send()
    for item in range(3):
        when(has_fw, lambda item=item: send2(item, True).wait_send())
        when(has_bw, lambda item=item: send2(item, False).wait_send())
    for half in range(2):
        for part in range(2):
            when(inner, lambda half=half, part=part: give(half, part).wait())
            when(outer, lambda half=half, part=part: keep(half, part).wait())


def local_call(quads, lower, upper, right_side):
    block = lower.shape[1:]
    half = (right_side.shape[2], right_side.shape[3])
    anywhere = pl.BlockSpec(memory_space=pl.ANY)
    dma = pltpu.SemaphoreType.DMA
    vmem = lambda *shape: pltpu.VMEM(shape, LOW)
    return pl.pallas_call(
        functools.partial(kernel, quads),
        out_shape=jax.ShapeDtypeStruct(right_side.shape, right_side.dtype),
        in_specs=[anywhere] * 3,
        out_specs=anywhere,
        scratch_shapes=[
            vmem(5, 2, *block),
            vmem(3, 2, *half),
            vmem(2, *block),
            vmem(2, *half),
            vmem(2, 2, *block),
            vmem(2, 2, *half),
            vmem(2, *block),
            vmem(2, *half),
            vmem(2, *block),
            vmem(2, 2, *half),
            vmem(2, *half),
            vmem(4, *block),
            vmem(2, *block),
            vmem(2, *block),
            vmem(2, *block),
            vmem(2, *block),
            dma((2,)),
            dma((2, 2)),
            dma((2, 4)),
            dma((2, 12)),
            dma((2, 2)),
            dma((2, 3, 2, 2)),
            dma((4,)),
            dma((4,)),
            dma((2, 4)),
            dma((2, 3)),
            dma((2, 3)),
            dma((2, 2, 2)),
        ],
        compiler_params=pltpu.CompilerParams(collective_id=0, has_side_effects=True),
    )(lower, upper, right_side)


def solution(mesh):
    placed = P(("energy", "chain"), None, None, None)
    return jax.shard_map(
        functools.partial(local_call, mesh.shape["chain"] // 4),
        mesh=mesh,
        in_specs=(placed,) * 3,
        out_specs=placed,
        check_vma=False,
    )
```

```python
import functools

import jax
import jax.numpy as jnp
from jax import lax
from jax.experimental import pallas as pl
from jax.experimental.pallas import tpu as pltpu
from jax.sharding import PartitionSpec as P

NS_STEPS = 2
MESH = pl.DeviceIdType.MESH
LOW = jnp.bfloat16

F, K = 0, 1
OWN, FW, BW = 0, 1, 2
SOWN, SFAR = 3, 4


def dot(left, right):
    return jnp.dot(left, right, preferred_element_type=jnp.float32)


def product(*pairs):
    left = jnp.concatenate([part for l, _ in pairs for part in (l[0], l[1])], axis=1)
    real = jnp.concatenate([part for _, r in pairs for part in (r[0], -r[1])], axis=0)
    imag = jnp.concatenate([part for _, r in pairs for part in (r[1], r[0])], axis=0)
    return dot(left, real), dot(left, imag)


def rhs_product(*pairs):
    left = jnp.concatenate([part for l, _ in pairs for part in (l[0], l[1])], axis=1)
    right = []
    for _, r in pairs:
        wide = r.shape[1] // 2
        right += [r, jnp.concatenate([-r[:, wide:], r[:, :wide]], axis=1)]
    return dot(left, jnp.concatenate(right, axis=0))


def rounded(parts):
    return jnp.stack([parts[0].astype(LOW), parts[1].astype(LOW)])


def negated(parts):
    return -parts[0], -parts[1]


def kernel(
    quads, l_ref, u_ref, b_ref, out_ref,
    u0, b0, own1, bown1, u1, b1, own2, bown2, u2, b2, last, inv, raw, side_raw, low, fix,
    sem_load, sem_bload, sem_m, sem_y, sem_d, sem_s,
    sem_1m, sem_1z, sem_1r, sem_2s, sem_2r, sem_out,
):
    me = lax.axis_index("chain")
    q = me // 4
    a = (me // 2) % 2
    b = me % 2
    inner = a != b
    outer = a == b
    qf, qb = q + 1 - 2 * a, q - 1 + 2 * a
    has_fw = (qf >= 0) & (qf < quads)
    has_bw = (qb >= 0) & (qb < quads)
    order = l_ref.shape[2]
    wide = b_ref.shape[3] // 2

    def at(quad, y, core):
        return {"chain": quad * 4 + y * 2 + core}

    mate = at(q, a, 1 - b)
    across = at(q, 1 - a, b)
    twin = at(q, b, a)
    fw, bw = at(qf, a, b), at(qb, a, b)
    side = {"chain": jnp.where(inner, at(qf, a, 1 - b)["chain"], at(qb, a, 1 - b)["chain"])}
    has_side = (inner & has_fw) | (outer & has_bw)
    diag = at(qb, 1 - a, 1 - b)
    has_diag = outer & has_bw

    def local(src, dst, sem):
        return pltpu.make_async_copy(src, dst, sem)

    def remote(src, dst, send, recv, who):
        return pltpu.make_async_remote_copy(
            src_ref=src, dst_ref=dst, send_sem=send, recv_sem=recv,
            device_id=who, device_id_type=MESH,
        )

    def arrive(ref, sem):
        pltpu.make_async_copy(ref, ref, sem).wait()

    def when(condition, action):
        pl.when(condition)(action)

    home = jnp.where(outer, OWN, BW)

    def load(unit):
        place = jnp.where(a == 0, 1 - unit, unit)
        return local((l_ref, u_ref)[unit].at[0], u0.at[home, place], sem_load.at[unit])

    def load_rhs(half, part):
        return local(
            b_ref.at[0, part, :, pl.ds(half * wide, wide)],
            b0.at[home, half, :, pl.ds(part * wide, wide)],
            sem_bload.at[half, part],
        )

    for unit in range(2):
        load(unit).start()
    for half in range(2):
        for part in range(2):
            load_rhs(half, part).start()

    barrier = pltpu.get_barrier_semaphore()

    def greet(who):
        pl.semaphore_signal(barrier, inc=1, device_id=who, device_id_type=MESH)

    greet(mate)
    greet(across)
    greetings = ((has_side, side), (has_diag, diag), (inner, twin), (has_fw, fw), (has_bw, bw))
    count = 2
    for exists, who in greetings:
        when(exists, functools.partial(greet, who))
        count = count + exists.astype(jnp.int32)

    def clear(ref):
        ref[...] = jnp.zeros(ref.shape, ref.dtype)

    has_one = {FW: outer | has_fw, BW: inner | has_bw}
    has_two = {FW: has_fw, BW: has_bw}

    @pl.when(outer & jnp.logical_not(has_bw))
    def _():
        clear(u0.at[BW])
        clear(b0.at[BW])

    @pl.when(jnp.logical_not(has_side))
    def _():
        clear(u0.at[SOWN])
        clear(u0.at[SFAR])

    for slot in (FW, BW):
        @pl.when(jnp.logical_not(has_one[slot]))
        def _():
            clear(b1.at[slot - 1])

        @pl.when(jnp.logical_not(has_two[slot]))
        def _():
            clear(u2.at[slot - 1])
            clear(b2.at[slot - 1])

    for unit in range(2):
        load(unit).wait()
    pl.semaphore_wait(barrier, count)

    def to_mate(item):
        if item < 2:
            src, dst = u0.at[BW, item], u0.at[FW, item]
        else:
            src, dst = b0.at[BW, item - 2], b0.at[FW, item - 2]
        return remote(src, dst, sem_m.at[0, item], sem_m.at[1, item], mate)

    def mate_in(item):
        ref = u0.at[FW, item] if item < 2 else b0.at[FW, item - 2]
        arrive(ref, sem_m.at[1, item])

    def y_place(item):
        if item < 8:
            return u0.at[FW if item < 4 else OWN, (item // 2) % 2, item % 2]
        return b0.at[FW if item < 10 else OWN, item % 2]

    def over_y(item):
        if item < 8:
            src = u0.at[OWN if item < 4 else FW, 1 - (item // 2) % 2, item % 2]
        else:
            src = b0.at[OWN if item < 10 else FW, item % 2]
        return remote(src, y_place(item), sem_y.at[0, item], sem_y.at[1, item], across)

    def y_in(item):
        arrive(y_place(item), sem_y.at[1, item])

    def to_side(source, place, unit, part):
        return remote(
            u0.at[source, unit, part], u0.at[place, unit, part],
            sem_s.at[0, place - BW, unit, part], sem_s.at[1, place - BW, unit, part], side,
        )

    def start_side(source, place, unit):
        for part in range(2):
            when(has_side, lambda part=part: to_side(source, place, unit, part).start())

    def side_in(place, unit):
        for part in range(2):
            ref, sem = u0.at[place, unit, part], sem_s.at[1, place - BW, unit, part]
            when(has_side, lambda ref=ref, sem=sem: arrive(ref, sem))

    def hand_on(item):
        y_in(item)
        source, place = (FW, BW) if item < 4 else (OWN, SOWN)
        when(has_side, lambda: to_side(source, place, (item // 2) % 2, item % 2).start())

    def over_diag(half):
        return remote(
            b0.at[OWN, half], b0.at[BW, half], sem_d.at[0, half], sem_d.at[1, half], diag
        )

    def wait_rhs():
        for half in range(2):
            for part in range(2):
                load_rhs(half, part).wait()

    row = lax.broadcasted_iota(jnp.int32, (order, order), 0)
    col = lax.broadcasted_iota(jnp.int32, (order, order), 1)
    unit_matrix = (row == col).astype(jnp.float32)

    def inverse(*jobs):
        for place, (off, number) in enumerate(jobs):
            low[place] = rounded((unit_matrix - off[0], -off[1]))
            inv[number] = rounded((unit_matrix + off[0], off[1]))
        for _ in range(NS_STEPS):
            for place, (_, number) in enumerate(jobs):
                prod = product((low[place], inv[number]))
                fix[place] = rounded((2.0 * unit_matrix - prod[0], -prod[1]))
            for place, (_, number) in enumerate(jobs):
                inv[number] = rounded(product((inv[number], fix[place])))

    def crossed(left, right):
        return rounded(negated(product((left, right))))

    def solved(number, right):
        return rounded(product((inv[number], right)))

    def new_rhs(number, own, k, f, behind, ahead):
        change = rhs_product((k, behind), (f, ahead))
        residual = (own.astype(jnp.float32) - change).astype(LOW)
        return rhs_product((inv[number], residual)).astype(LOW)

    mate_slot = jnp.where(outer, BW - 1, FW - 1)
    side_slot = jnp.where(outer, FW - 1, BW - 1)

    def send1(item, slot, sem, who):
        if item < 2:
            src, dst = own1.at[item], u1.at[slot, item]
        else:
            src, dst = bown1.at[item - 2], b1.at[slot, item - 2]
        return remote(src, dst, sem.at[item], sem_1r.at[slot, item], who)

    def to_side1(item):
        return send1(item, side_slot, sem_1z, side)

    def to_mate1(item):
        return send1(item, mate_slot, sem_1m, mate)

    def start1(item):
        if item >= 2:
            when(has_side, lambda: to_side1(item).start())
        to_mate1(item).start()

    def in1(slot, item):
        ref = u1.at[slot - 1, item] if item < 2 else b1.at[slot - 1, item - 2]
        when(has_one[slot], lambda: arrive(ref, sem_1r.at[slot - 1, item]))

    def send2(item, ahead):
        slot = (BW if ahead else FW) - 1
        if item == 0:
            src, dst = own2.at[F if ahead else K], u2.at[slot]
        else:
            src, dst = bown2.at[item - 1], b2.at[slot, item - 1]
        way = 0 if ahead else 1
        return remote(
            src, dst, sem_2s.at[way, item], sem_2r.at[slot, item], fw if ahead else bw
        )

    def start2(item, ahead):
        when(has_fw if ahead else has_bw, lambda: send2(item, ahead).start())

    def in2(slot, item):
        ref = u2.at[slot - 1] if item == 0 else b2.at[slot - 1, item - 1]
        when(has_two[slot], lambda: arrive(ref, sem_2r.at[slot - 1, item]))

    def rhs0():
        for half in range(2):
            @pl.when(inner)
            def _():
                y_in(8 + half)
                y_in(10 + half)

            when(has_diag, lambda: arrive(b0.at[BW, half], sem_d.at[1, half]))
            bown1[half] = new_rhs(
                0, b0[OWN, half], u0[OWN, K], u0[OWN, F], b0[BW, half], b0[FW, half]
            )
            start1(2 + half)

    def inverse1():
        inverse((product((own1[K], u1[BW - 1, F]), (own1[F], u1[FW - 1, K])), 1))

    def cross1(unit):
        slot = FW if unit == F else BW
        raw[unit] = crossed(own1[unit], u1[slot - 1, unit])

    @pl.when(inner)
    def _():
        to_mate(K).start()
        to_mate(F).start()
        start_side(BW, SFAR, F)
        wait_rhs()
        for half in range(2):
            to_mate(2 + half).start()
        for item in range(4):
            hand_on(item)
        side_in(SOWN, K)
        side_raw[K] = crossed(u0[SOWN, K], u0[FW, K])
        for item in (4, 5):
            hand_on(item)
        side_in(SOWN, F)
        side_in(SFAR, K)
        inverse((product((u0[SOWN, K], u0[FW, F]), (u0[SOWN, F], u0[SFAR, K])), 3))
        raw[F] = crossed(u0[OWN, F], u0[FW, F])
        u1[FW - 1, K] = solved(3, side_raw[K])
        for item in (6, 7):
            hand_on(item)
        start_side(BW, SFAR, K)
        inverse((product((u0[OWN, K], u0[BW, F]), (u0[OWN, F], u0[FW, K])), 0))
        raw[K] = crossed(u0[OWN, K], u0[BW, K])
        own1[F] = solved(0, raw[F])
        own1[K] = solved(0, raw[K])
        start1(F)
        start1(K)
        side_in(SFAR, F)
        in1(BW, F)
        in1(BW, K)
        inverse1()
        side_raw[F] = crossed(u0[SOWN, F], u0[SFAR, F])
        u1[FW - 1, F] = solved(3, side_raw[F])
        for unit in (F, K):
            cross1(unit)
        for unit in (F, K):
            own2[unit] = solved(1, raw[unit])
        start2(0, True)
        start2(0, False)
        rhs0()

    @pl.when(outer)
    def _():
        for item in range(4):
            over_y(item).start()
        start_side(OWN, SOWN, K)
        start_side(OWN, SOWN, F)
        mate_in(K)
        for item in (4, 5):
            over_y(item).start()
        start_side(FW, SFAR, K)
        mate_in(F)
        for item in (6, 7):
            over_y(item).start()
        start_side(FW, SFAR, F)
        wait_rhs()
        for half in range(2):
            over_y(8 + half).start()
            mate_in(2 + half)
            over_y(10 + half).start()
        raw[F] = crossed(u0[OWN, F], u0[FW, F])
        side_in(BW, F)
        inverse((product((u0[OWN, K], u0[BW, F]), (u0[OWN, F], u0[FW, K])), 0))
        own1[F] = solved(0, raw[F])
        start1(F)
        side_in(BW, K)
        raw[K] = crossed(u0[OWN, K], u0[BW, K])
        own1[K] = solved(0, raw[K])
        start1(K)
        for item in (6, 7):
            over_y(item).wait_send()
        for half in range(2):
            when(has_bw, lambda half=half: over_diag(half).start())
        side_in(SOWN, F)
        side_raw[F] = crossed(u0[SOWN, F], u0[BW, F])
        in1(FW, F)
        in1(FW, K)
        cross1(F)
        side_in(SFAR, F)
        side_in(SOWN, K)
        inverse((product((u0[SOWN, K], u0[SFAR, F]), (u0[SOWN, F], u0[BW, K])), 3))
        u1[BW - 1, F] = solved(3, side_raw[F])
        inverse1()
        own2[F] = solved(1, raw[F])
        start2(0, True)
        rhs0()
        side_in(SFAR, K)
        side_raw[K] = crossed(u0[SOWN, K], u0[SFAR, K])
        u1[BW - 1, K] = solved(3, side_raw[K])
        cross1(K)
        own2[K] = solved(1, raw[K])
        start2(0, False)

    for half in range(2):
        in1(FW, 2 + half)
        in1(BW, 2 + half)
        bown2[half] = new_rhs(
            1, bown1[half], own1[K], own1[F], b1[BW - 1, half], b1[FW - 1, half]
        )
        start2(1 + half, True)
        start2(1 + half, False)

    def spot(half, part):
        return (
            last.at[half, :, pl.ds(part * wide, wide)],
            out_ref.at[0, part, :, pl.ds(half * wide, wide)],
        )

    def give(half, part):
        src, dst = spot(half, part)
        return remote(src, dst, sem_out.at[0, half, part], sem_out.at[1, half, part], twin)

    def keep(half, part):
        src, dst = spot(half, part)
        return local(src, dst, sem_out.at[1, half, part])

    in2(FW, 0)
    in2(BW, 0)
    inverse((product((own2[K], u2[BW - 1]), (own2[F], u2[FW - 1])), 2))
    for half in range(2):
        in2(FW, 1 + half)
        in2(BW, 1 + half)
        last[half] = new_rhs(
            2, bown2[half], own2[K], own2[F], b2[BW - 1, half], b2[FW - 1, half]
        )
        for part in range(2):
            when(inner, lambda half=half, part=part: give(half, part).start())
            when(outer, lambda half=half, part=part: keep(half, part).start())

    @pl.when(inner)
    def _():
        for item in range(4):
            to_mate(item).wait_send()

    @pl.when(outer)
    def _():
        for item in range(12):
            if item not in (6, 7):
                over_y(item).wait_send()
        for half in range(2):
            when(has_bw, lambda half=half: over_diag(half).wait_send())

    def side_sent(source, place):
        for unit in range(2):
            for part in range(2):
                to_side(source, place, unit, part).wait_send()

    @pl.when(inner & has_side)
    def _():
        side_sent(FW, BW)
        side_sent(OWN, SOWN)
        side_sent(BW, SFAR)

    @pl.when(outer & has_side)
    def _():
        side_sent(OWN, SOWN)
        side_sent(FW, SFAR)

    for item in range(4):
        if item >= 2:
            when(has_side, lambda item=item: to_side1(item).wait_send())
        to_mate1(item).wait_send()
    for item in range(3):
        when(has_fw, lambda item=item: send2(item, True).wait_send())
        when(has_bw, lambda item=item: send2(item, False).wait_send())
    for half in range(2):
        for part in range(2):
            when(inner, lambda half=half, part=part: give(half, part).wait())
            when(outer, lambda half=half, part=part: keep(half, part).wait())


def local_call(quads, lower, upper, right_side):
    block = lower.shape[1:]
    half = (right_side.shape[2], right_side.shape[3])
    anywhere = pl.BlockSpec(memory_space=pl.ANY)
    dma = pltpu.SemaphoreType.DMA
    vmem = lambda *shape: pltpu.VMEM(shape, LOW)
    return pl.pallas_call(
        functools.partial(kernel, quads),
        out_shape=jax.ShapeDtypeStruct(right_side.shape, right_side.dtype),
        in_specs=[anywhere] * 3,
        out_specs=anywhere,
        scratch_shapes=[
            vmem(5, 2, *block),
            vmem(3, 2, *half),
            vmem(2, *block),
            vmem(2, *half),
            vmem(2, 2, *block),
            vmem(2, 2, *half),
            vmem(2, *block),
            vmem(2, *half),
            vmem(2, *block),
            vmem(2, 2, *half),
            vmem(2, *half),
            vmem(4, *block),
            vmem(2, *block),
            vmem(2, *block),
            vmem(2, *block),
            vmem(2, *block),
            dma((2,)),
            dma((2, 2)),
            dma((2, 4)),
            dma((2, 12)),
            dma((2, 2)),
            dma((2, 3, 2, 2)),
            dma((4,)),
            dma((4,)),
            dma((2, 4)),
            dma((2, 3)),
            dma((2, 3)),
            dma((2, 2, 2)),
        ],
        compiler_params=pltpu.CompilerParams(collective_id=0, has_side_effects=True),
    )(lower, upper, right_side)


def solution(mesh):
    placed = P(("energy", "chain"), None, None, None)
    return jax.shard_map(
        functools.partial(local_call, mesh.shape["chain"] // 4),
        mesh=mesh,
        in_specs=(placed,) * 3,
        out_specs=placed,
        check_vma=False,
    )
```

```python
import functools

import jax
import jax.numpy as jnp
from jax import lax
from jax.experimental import pallas as pl
from jax.experimental.pallas import tpu as pltpu
from jax.sharding import PartitionSpec as P

NS_STEPS = 2
MESH = pl.DeviceIdType.MESH
LOW = jnp.bfloat16

F, K = 0, 1
OWN, FW, BW = 0, 1, 2
SOWN, SFAR = 3, 4


def dot(left, right):
    return jnp.dot(left, right, preferred_element_type=jnp.float32)


def product(*pairs):
    left = jnp.concatenate([part for l, _ in pairs for part in (l[0], l[1])], axis=1)
    real = jnp.concatenate([part for _, r in pairs for part in (r[0], -r[1])], axis=0)
    imag = jnp.concatenate([part for _, r in pairs for part in (r[1], r[0])], axis=0)
    return dot(left, real), dot(left, imag)


def rhs_product(*pairs):
    left = jnp.concatenate([part for l, _ in pairs for part in (l[0], l[1])], axis=1)
    right = []
    for _, r in pairs:
        wide = r.shape[1] // 2
        right += [r, jnp.concatenate([-r[:, wide:], r[:, :wide]], axis=1)]
    return dot(left, jnp.concatenate(right, axis=0))


def rounded(parts):
    return jnp.stack([parts[0].astype(LOW), parts[1].astype(LOW)])


def negated(parts):
    return -parts[0], -parts[1]


def kernel(
    quads, l_ref, u_ref, b_ref, out_ref,
    u0, b0, own1, bown1, u1, b1, own2, bown2, u2, b2, last, inv, raw, side_raw, low, fix, partial,
    sem_load, sem_bload, sem_m, sem_y, sem_d, sem_s,
    sem_1m, sem_1z, sem_1r, sem_2s, sem_2r, sem_out,
):
    me = lax.axis_index("chain")
    q = me // 4
    a = (me // 2) % 2
    b = me % 2
    inner = a != b
    outer = a == b
    qf, qb = q + 1 - 2 * a, q - 1 + 2 * a
    has_fw = (qf >= 0) & (qf < quads)
    has_bw = (qb >= 0) & (qb < quads)
    order = l_ref.shape[2]
    wide = b_ref.shape[3] // 2

    def at(quad, y, core):
        return {"chain": quad * 4 + y * 2 + core}

    mate = at(q, a, 1 - b)
    across = at(q, 1 - a, b)
    twin = at(q, b, a)
    fw, bw = at(qf, a, b), at(qb, a, b)
    side = {"chain": jnp.where(inner, at(qf, a, 1 - b)["chain"], at(qb, a, 1 - b)["chain"])}
    has_side = (inner & has_fw) | (outer & has_bw)
    diag = at(qb, 1 - a, 1 - b)
    has_diag = outer & has_bw

    def local(src, dst, sem):
        return pltpu.make_async_copy(src, dst, sem)

    def remote(src, dst, send, recv, who):
        return pltpu.make_async_remote_copy(
            src_ref=src, dst_ref=dst, send_sem=send, recv_sem=recv,
            device_id=who, device_id_type=MESH,
        )

    def arrive(ref, sem):
        pltpu.make_async_copy(ref, ref, sem).wait()

    def when(condition, action):
        pl.when(condition)(action)

    home = jnp.where(outer, OWN, BW)

    def load(unit):
        place = jnp.where(a == 0, 1 - unit, unit)
        return local((l_ref, u_ref)[unit].at[0], u0.at[home, place], sem_load.at[unit])

    def load_rhs(half, part):
        return local(
            b_ref.at[0, part, :, pl.ds(half * wide, wide)],
            b0.at[home, half, :, pl.ds(part * wide, wide)],
            sem_bload.at[half, part],
        )

    for unit in range(2):
        load(unit).start()
    for half in range(2):
        for part in range(2):
            load_rhs(half, part).start()

    barrier = pltpu.get_barrier_semaphore()

    def greet(who):
        pl.semaphore_signal(barrier, inc=1, device_id=who, device_id_type=MESH)

    greet(mate)
    greet(across)
    greetings = ((has_side, side), (has_diag, diag), (inner, twin), (has_fw, fw), (has_bw, bw))
    count = 2
    for exists, who in greetings:
        when(exists, functools.partial(greet, who))
        count = count + exists.astype(jnp.int32)

    def clear(ref):
        ref[...] = jnp.zeros(ref.shape, ref.dtype)

    has_one = {FW: outer | has_fw, BW: inner | has_bw}
    has_two = {FW: has_fw, BW: has_bw}

    @pl.when(outer & jnp.logical_not(has_bw))
    def _():
        clear(u0.at[BW])
        clear(b0.at[BW])

    @pl.when(jnp.logical_not(has_side))
    def _():
        clear(u0.at[SOWN])
        clear(u0.at[SFAR])

    for slot in (FW, BW):
        @pl.when(jnp.logical_not(has_one[slot]))
        def _():
            clear(b1.at[slot - 1])

        @pl.when(jnp.logical_not(has_two[slot]))
        def _():
            clear(u2.at[slot - 1])
            clear(b2.at[slot - 1])

    for unit in range(2):
        load(unit).wait()
    pl.semaphore_wait(barrier, count)

    def to_mate(item):
        if item < 2:
            src, dst = u0.at[BW, item], u0.at[FW, item]
        else:
            src, dst = b0.at[BW, item - 2], b0.at[FW, item - 2]
        return remote(src, dst, sem_m.at[0, item], sem_m.at[1, item], mate)

    def mate_in(item):
        ref = u0.at[FW, item] if item < 2 else b0.at[FW, item - 2]
        arrive(ref, sem_m.at[1, item])

    def y_place(item):
        if item < 8:
            return u0.at[FW if item < 4 else OWN, (item // 2) % 2, item % 2]
        return b0.at[OWN, item % 2]

    def over_y(item):
        if item < 8:
            src = u0.at[OWN if item < 4 else FW, 1 - (item // 2) % 2, item % 2]
        else:
            src = partial.at[item % 2]
        return remote(src, y_place(item), sem_y.at[0, item], sem_y.at[1, item], across)

    def y_in(item):
        arrive(y_place(item), sem_y.at[1, item])

    def to_side(source, place, unit, part):
        return remote(
            u0.at[source, unit, part], u0.at[place, unit, part],
            sem_s.at[0, place - BW, unit, part], sem_s.at[1, place - BW, unit, part], side,
        )

    def start_side(source, place, unit):
        for part in range(2):
            when(has_side, lambda part=part: to_side(source, place, unit, part).start())

    def side_in(place, unit):
        for part in range(2):
            ref, sem = u0.at[place, unit, part], sem_s.at[1, place - BW, unit, part]
            when(has_side, lambda ref=ref, sem=sem: arrive(ref, sem))

    def hand_on(item):
        y_in(item)
        source, place = (FW, BW) if item < 4 else (OWN, SOWN)
        when(has_side, lambda: to_side(source, place, (item // 2) % 2, item % 2).start())

    def over_diag(half):
        return remote(
            b0.at[OWN, half], b0.at[BW, half], sem_d.at[0, half], sem_d.at[1, half], diag
        )

    def wait_rhs():
        for half in range(2):
            for part in range(2):
                load_rhs(half, part).wait()

    row = lax.broadcasted_iota(jnp.int32, (order, order), 0)
    col = lax.broadcasted_iota(jnp.int32, (order, order), 1)
    unit_matrix = (row == col).astype(jnp.float32)

    def inverse(*jobs):
        for place, (off, number) in enumerate(jobs):
            low[place] = rounded((unit_matrix - off[0], -off[1]))
            inv[number] = rounded((unit_matrix + off[0], off[1]))
        for _ in range(NS_STEPS):
            for place, (_, number) in enumerate(jobs):
                prod = product((low[place], inv[number]))
                fix[place] = rounded((2.0 * unit_matrix - prod[0], -prod[1]))
            for place, (_, number) in enumerate(jobs):
                inv[number] = rounded(product((inv[number], fix[place])))

    def crossed(left, right):
        return rounded(negated(product((left, right))))

    def solved(number, right):
        return rounded(product((inv[number], right)))

    def residual(own, *pairs):
        return (own.astype(jnp.float32) - rhs_product(*pairs)).astype(LOW)

    def new_rhs(number, own, *pairs):
        return rhs_product((inv[number], residual(own, *pairs))).astype(LOW)

    mate_slot = jnp.where(outer, BW - 1, FW - 1)
    side_slot = jnp.where(outer, FW - 1, BW - 1)

    def send1(item, slot, sem, who):
        if item < 2:
            src, dst = own1.at[item], u1.at[slot, item]
        else:
            src, dst = bown1.at[item - 2], b1.at[slot, item - 2]
        return remote(src, dst, sem.at[item], sem_1r.at[slot, item], who)

    def to_side1(item):
        return send1(item, side_slot, sem_1z, side)

    def to_mate1(item):
        return send1(item, mate_slot, sem_1m, mate)

    def start1(item):
        if item >= 2:
            when(has_side, lambda: to_side1(item).start())
        to_mate1(item).start()

    def in1(slot, item):
        ref = u1.at[slot - 1, item] if item < 2 else b1.at[slot - 1, item - 2]
        when(has_one[slot], lambda: arrive(ref, sem_1r.at[slot - 1, item]))

    def send2(item, ahead):
        slot = (BW if ahead else FW) - 1
        if item == 0:
            src, dst = own2.at[F if ahead else K], u2.at[slot]
        else:
            src, dst = bown2.at[item - 1], b2.at[slot, item - 1]
        way = 0 if ahead else 1
        return remote(
            src, dst, sem_2s.at[way, item], sem_2r.at[slot, item], fw if ahead else bw
        )

    def start2(item, ahead):
        when(has_fw if ahead else has_bw, lambda: send2(item, ahead).start())

    def in2(slot, item):
        ref = u2.at[slot - 1] if item == 0 else b2.at[slot - 1, item - 1]
        when(has_two[slot], lambda: arrive(ref, sem_2r.at[slot - 1, item]))

    def rhs0(half, *pairs):
        bown1[half] = new_rhs(0, b0[OWN, half], (u0[OWN, K], b0[BW, half]), *pairs)
        start1(2 + half)

    def inner_rhs0(half):
        y_in(8 + half)
        rhs0(half)

    def outer_rhs0(half):
        when(has_bw, lambda: arrive(b0.at[BW, half], sem_d.at[1, half]))
        rhs0(half, (u0[OWN, F], b0[FW, half]))

    def rhs1(half):
        bown2[half] = new_rhs(
            1, bown1[half], (own1[K], b1[BW - 1, half]), (own1[F], b1[FW - 1, half])
        )
        start2(1 + half, True)
        start2(1 + half, False)

    def inverse1():
        inverse((product((own1[K], u1[BW - 1, F]), (own1[F], u1[FW - 1, K])), 1))

    def cross1(unit):
        slot = FW if unit == F else BW
        raw[unit] = crossed(own1[unit], u1[slot - 1, unit])

    @pl.when(inner)
    def _():
        to_mate(K).start()
        to_mate(F).start()
        start_side(BW, SFAR, F)
        wait_rhs()
        for half in range(2):
            to_mate(2 + half).start()
        for item in range(4):
            hand_on(item)
        side_in(SOWN, K)
        side_raw[K] = crossed(u0[SOWN, K], u0[FW, K])
        for item in (4, 5):
            hand_on(item)
        side_in(SOWN, F)
        side_in(SFAR, K)
        inverse((product((u0[SOWN, K], u0[FW, F]), (u0[SOWN, F], u0[SFAR, K])), 3))
        raw[F] = crossed(u0[OWN, F], u0[FW, F])
        u1[FW - 1, K] = solved(3, side_raw[K])
        for item in (6, 7):
            hand_on(item)
        start_side(BW, SFAR, K)
        inverse((product((u0[OWN, K], u0[BW, F]), (u0[OWN, F], u0[FW, K])), 0))
        raw[K] = crossed(u0[OWN, K], u0[BW, K])
        own1[F] = solved(0, raw[F])
        own1[K] = solved(0, raw[K])
        start1(F)
        start1(K)
        side_in(SFAR, F)
        in1(BW, F)
        in1(BW, K)
        inverse1()
        side_raw[F] = crossed(u0[SOWN, F], u0[SFAR, F])
        u1[FW - 1, F] = solved(3, side_raw[F])
        for unit in (F, K):
            cross1(unit)
        for unit in (F, K):
            own2[unit] = solved(1, raw[unit])
        start2(0, True)
        start2(0, False)
        for half in range(2):
            inner_rhs0(half)
        for half in range(2):
            in1(FW, 2 + half)
            in1(BW, 2 + half)
            rhs1(half)

    @pl.when(outer)
    def _():
        for item in range(4):
            over_y(item).start()
        start_side(OWN, SOWN, K)
        start_side(OWN, SOWN, F)
        mate_in(K)
        for item in (4, 5):
            over_y(item).start()
        start_side(FW, SFAR, K)
        mate_in(F)
        for item in (6, 7):
            over_y(item).start()
        start_side(FW, SFAR, F)
        wait_rhs()
        for half in range(2):
            mate_in(2 + half)
            partial[half] = residual(b0[FW, half], (u0[FW, K], b0[OWN, half]))
        raw[F] = crossed(u0[OWN, F], u0[FW, F])
        side_in(BW, F)
        inverse((product((u0[OWN, K], u0[BW, F]), (u0[OWN, F], u0[FW, K])), 0))
        own1[F] = solved(0, raw[F])
        start1(F)
        side_in(BW, K)
        raw[K] = crossed(u0[OWN, K], u0[BW, K])
        own1[K] = solved(0, raw[K])
        start1(K)
        for item in (6, 7):
            over_y(item).wait_send()
        for half in range(2):
            when(has_bw, lambda half=half: over_diag(half).start())
        when(has_bw, lambda: over_diag(0).wait_send())
        for item in (8, 9):
            over_y(item).start()
        side_in(SOWN, F)
        side_raw[F] = crossed(u0[SOWN, F], u0[BW, F])
        in1(FW, F)
        in1(FW, K)
        cross1(F)
        outer_rhs0(0)
        side_in(SFAR, F)
        side_in(SOWN, K)
        inverse((product((u0[SOWN, K], u0[SFAR, F]), (u0[SOWN, F], u0[BW, K])), 3))
        u1[BW - 1, F] = solved(3, side_raw[F])
        outer_rhs0(1)
        inverse1()
        own2[F] = solved(1, raw[F])
        side_in(SFAR, K)
        side_raw[K] = crossed(u0[SOWN, K], u0[SFAR, K])
        u1[BW - 1, K] = solved(3, side_raw[K])
        cross1(K)
        own2[K] = solved(1, raw[K])
        start2(0, False)
        in1(FW, 2)
        in1(BW, 2)
        rhs1(0)
        start2(0, True)
        in1(FW, 3)
        in1(BW, 3)
        rhs1(1)

    def spot(half, part):
        return (
            last.at[half, :, pl.ds(part * wide, wide)],
            out_ref.at[0, part, :, pl.ds(half * wide, wide)],
        )

    def give(half, part):
        src, dst = spot(half, part)
        return remote(src, dst, sem_out.at[0, half, part], sem_out.at[1, half, part], twin)

    def keep(half, part):
        src, dst = spot(half, part)
        return local(src, dst, sem_out.at[1, half, part])

    in2(FW, 0)
    in2(BW, 0)
    inverse((product((own2[K], u2[BW - 1]), (own2[F], u2[FW - 1])), 2))
    for half in range(2):
        in2(FW, 1 + half)
        in2(BW, 1 + half)
        last[half] = new_rhs(
            2, bown2[half], (own2[K], b2[BW - 1, half]), (own2[F], b2[FW - 1, half])
        )
        for part in range(2):
            when(inner, lambda half=half, part=part: give(half, part).start())
            when(outer, lambda half=half, part=part: keep(half, part).start())

    @pl.when(inner)
    def _():
        for item in range(4):
            to_mate(item).wait_send()

    @pl.when(outer)
    def _():
        for item in range(10):
            if item not in (6, 7):
                over_y(item).wait_send()
        when(has_bw, lambda: over_diag(1).wait_send())

    def side_sent(source, place):
        for unit in range(2):
            for part in range(2):
                to_side(source, place, unit, part).wait_send()

    @pl.when(inner & has_side)
    def _():
        side_sent(FW, BW)
        side_sent(OWN, SOWN)
        side_sent(BW, SFAR)

    @pl.when(outer & has_side)
    def _():
        side_sent(OWN, SOWN)
        side_sent(FW, SFAR)

    for item in range(4):
        if item >= 2:
            when(has_side, lambda item=item: to_side1(item).wait_send())
        to_mate1(item).wait_send()
    for item in range(3):
        when(has_fw, lambda item=item: send2(item, True).wait_send())
        when(has_bw, lambda item=item: send2(item, False).wait_send())
    for half in range(2):
        for part in range(2):
            when(inner, lambda half=half, part=part: give(half, part).wait())
            when(outer, lambda half=half, part=part: keep(half, part).wait())


def local_call(quads, lower, upper, right_side):
    block = lower.shape[1:]
    half = (right_side.shape[2], right_side.shape[3])
    anywhere = pl.BlockSpec(memory_space=pl.ANY)
    dma = pltpu.SemaphoreType.DMA
    vmem = lambda *shape: pltpu.VMEM(shape, LOW)
    return pl.pallas_call(
        functools.partial(kernel, quads),
        out_shape=jax.ShapeDtypeStruct(right_side.shape, right_side.dtype),
        in_specs=[anywhere] * 3,
        out_specs=anywhere,
        scratch_shapes=[
            vmem(5, 2, *block),
            vmem(3, 2, *half),
            vmem(2, *block),
            vmem(2, *half),
            vmem(2, 2, *block),
            vmem(2, 2, *half),
            vmem(2, *block),
            vmem(2, *half),
            vmem(2, *block),
            vmem(2, 2, *half),
            vmem(2, *half),
            vmem(4, *block),
            vmem(2, *block),
            vmem(2, *block),
            vmem(2, *block),
            vmem(2, *block),
            vmem(2, *half),
            dma((2,)),
            dma((2, 2)),
            dma((2, 4)),
            dma((2, 10)),
            dma((2, 2)),
            dma((2, 3, 2, 2)),
            dma((4,)),
            dma((4,)),
            dma((2, 4)),
            dma((2, 3)),
            dma((2, 3)),
            dma((2, 2, 2)),
        ],
        compiler_params=pltpu.CompilerParams(collective_id=0, has_side_effects=True),
    )(lower, upper, right_side)


def solution(mesh):
    placed = P(("energy", "chain"), None, None, None)
    return jax.shard_map(
        functools.partial(local_call, mesh.shape["chain"] // 4),
        mesh=mesh,
        in_specs=(placed,) * 3,
        out_specs=placed,
        check_vma=False,
    )
```

```python
import functools

import jax
import jax.numpy as jnp
from jax import lax
from jax.experimental import pallas as pl
from jax.experimental.pallas import tpu as pltpu
from jax.sharding import PartitionSpec as P

NS_STEPS = 2
MESH = pl.DeviceIdType.MESH
LOW = jnp.bfloat16

F, K = 0, 1
OWN, FW, BW = 0, 1, 2
SOWN, SFAR = 3, 4


def dot(left, right):
    return jnp.dot(left, right, preferred_element_type=jnp.float32)


def product(*pairs):
    left = jnp.concatenate([part for l, _ in pairs for part in (l[0], l[1])], axis=1)
    real = jnp.concatenate([part for _, r in pairs for part in (r[0], -r[1])], axis=0)
    imag = jnp.concatenate([part for _, r in pairs for part in (r[1], r[0])], axis=0)
    return dot(left, real), dot(left, imag)


def rhs_product(*pairs):
    left = jnp.concatenate([part for l, _ in pairs for part in (l[0], l[1])], axis=1)
    right = []
    for _, r in pairs:
        wide = r.shape[1] // 2
        right += [r, jnp.concatenate([-r[:, wide:], r[:, :wide]], axis=1)]
    return dot(left, jnp.concatenate(right, axis=0))


def rounded(parts):
    return jnp.stack([parts[0].astype(LOW), parts[1].astype(LOW)])


def negated(parts):
    return -parts[0], -parts[1]


def kernel(
    quads, l_ref, u_ref, b_ref, out_ref,
    u0, b0, own1, bown1, u1, b1, own2, bown2, u2, b2, last, inv, raw, side_raw, low, fix, partial,
    sem_load, sem_bload, sem_m, sem_y, sem_d, sem_s,
    sem_1m, sem_1z, sem_1r, sem_2s, sem_2r, sem_out,
):
    me = lax.axis_index("chain")
    q = me // 4
    a = (me // 2) % 2
    b = me % 2
    inner = a != b
    outer = a == b
    qf, qb = q + 1 - 2 * a, q - 1 + 2 * a
    has_fw = (qf >= 0) & (qf < quads)
    has_bw = (qb >= 0) & (qb < quads)
    order = l_ref.shape[2]
    wide = b_ref.shape[3] // 2

    def at(quad, y, core):
        return {"chain": quad * 4 + y * 2 + core}

    mate = at(q, a, 1 - b)
    across = at(q, 1 - a, b)
    twin = at(q, b, a)
    fw, bw = at(qf, a, b), at(qb, a, b)
    side = {"chain": jnp.where(inner, at(qf, a, 1 - b)["chain"], at(qb, a, 1 - b)["chain"])}
    has_side = (inner & has_fw) | (outer & has_bw)
    diag = at(qb, 1 - a, 1 - b)
    has_diag = outer & has_bw

    def local(src, dst, sem):
        return pltpu.make_async_copy(src, dst, sem)

    def remote(src, dst, send, recv, who):
        return pltpu.make_async_remote_copy(
            src_ref=src, dst_ref=dst, send_sem=send, recv_sem=recv,
            device_id=who, device_id_type=MESH,
        )

    def arrive(ref, sem):
        pltpu.make_async_copy(ref, ref, sem).wait()

    def when(condition, action):
        pl.when(condition)(action)

    home = jnp.where(outer, OWN, BW)

    def load(unit):
        place = jnp.where(a == 0, 1 - unit, unit)
        return local((l_ref, u_ref)[unit].at[0], u0.at[home, place], sem_load.at[unit])

    def load_rhs(half, part):
        return local(
            b_ref.at[0, part, :, pl.ds(half * wide, wide)],
            b0.at[home, half, :, pl.ds(part * wide, wide)],
            sem_bload.at[half, part],
        )

    for unit in range(2):
        load(unit).start()
    for half in range(2):
        for part in range(2):
            load_rhs(half, part).start()

    barrier = pltpu.get_barrier_semaphore()

    def greet(who):
        pl.semaphore_signal(barrier, inc=1, device_id=who, device_id_type=MESH)

    greet(mate)
    greet(across)
    greetings = ((has_side, side), (has_diag, diag), (inner, twin), (has_fw, fw), (has_bw, bw))
    count = 2
    for exists, who in greetings:
        when(exists, functools.partial(greet, who))
        count = count + exists.astype(jnp.int32)

    def clear(ref):
        ref[...] = jnp.zeros(ref.shape, ref.dtype)

    has_one = {FW: outer | has_fw, BW: inner | has_bw}
    has_two = {FW: has_fw, BW: has_bw}

    @pl.when(outer & jnp.logical_not(has_bw))
    def _():
        clear(u0.at[BW])
        clear(b0.at[BW])

    @pl.when(jnp.logical_not(has_side))
    def _():
        clear(u0.at[SOWN])
        clear(u0.at[SFAR])

    for slot in (FW, BW):
        @pl.when(jnp.logical_not(has_one[slot]))
        def _():
            clear(b1.at[slot - 1])

        @pl.when(jnp.logical_not(has_two[slot]))
        def _():
            clear(u2.at[slot - 1])
            clear(b2.at[slot - 1])

    for unit in range(2):
        load(unit).wait()
    pl.semaphore_wait(barrier, count)

    def to_mate(item):
        if item < 2:
            src, dst = u0.at[BW, item], u0.at[FW, item]
        else:
            src, dst = b0.at[BW, item - 2], b0.at[FW, item - 2]
        return remote(src, dst, sem_m.at[0, item], sem_m.at[1, item], mate)

    def mate_in(item):
        ref = u0.at[FW, item] if item < 2 else b0.at[FW, item - 2]
        arrive(ref, sem_m.at[1, item])

    def y_place(item):
        if item < 8:
            return u0.at[FW if item < 4 else OWN, (item // 2) % 2, item % 2]
        return b0.at[OWN, item % 2]

    def over_y(item):
        if item < 8:
            src = u0.at[OWN if item < 4 else FW, 1 - (item // 2) % 2, item % 2]
        else:
            src = partial.at[item % 2]
        return remote(src, y_place(item), sem_y.at[0, item], sem_y.at[1, item], across)

    def y_in(item):
        arrive(y_place(item), sem_y.at[1, item])

    def to_side(source, place, unit, part):
        return remote(
            u0.at[source, unit, part], u0.at[place, unit, part],
            sem_s.at[0, place - BW, unit, part], sem_s.at[1, place - BW, unit, part], side,
        )

    def start_side(source, place, unit):
        for part in range(2):
            when(has_side, lambda part=part: to_side(source, place, unit, part).start())

    def side_in(place, unit):
        for part in range(2):
            ref, sem = u0.at[place, unit, part], sem_s.at[1, place - BW, unit, part]
            when(has_side, lambda ref=ref, sem=sem: arrive(ref, sem))

    def hand_on(item):
        y_in(item)
        source, place = (FW, BW) if item < 4 else (OWN, SOWN)
        when(has_side, lambda: to_side(source, place, (item // 2) % 2, item % 2).start())

    def over_diag(half):
        return remote(
            b0.at[OWN, half], b0.at[BW, half], sem_d.at[0, half], sem_d.at[1, half], diag
        )

    def wait_rhs():
        for half in range(2):
            for part in range(2):
                load_rhs(half, part).wait()

    row = lax.broadcasted_iota(jnp.int32, (order, order), 0)
    col = lax.broadcasted_iota(jnp.int32, (order, order), 1)
    unit_matrix = (row == col).astype(jnp.float32)

    def inverse(*jobs):
        for place, (off, number) in enumerate(jobs):
            low[place] = rounded((unit_matrix - off[0], -off[1]))
            inv[number] = rounded((unit_matrix + off[0], off[1]))
        for _ in range(NS_STEPS):
            for place, (_, number) in enumerate(jobs):
                prod = product((low[place], inv[number]))
                fix[place] = rounded((2.0 * unit_matrix - prod[0], -prod[1]))
            for place, (_, number) in enumerate(jobs):
                inv[number] = rounded(product((inv[number], fix[place])))

    def crossed(left, right):
        return rounded(negated(product((left, right))))

    def solved(number, right):
        return rounded(product((inv[number], right)))

    def residual(own, *pairs):
        return (own.astype(jnp.float32) - rhs_product(*pairs)).astype(LOW)

    def new_rhs(number, own, *pairs):
        return rhs_product((inv[number], residual(own, *pairs))).astype(LOW)

    mate_slot = jnp.where(outer, BW - 1, FW - 1)
    side_slot = jnp.where(outer, FW - 1, BW - 1)

    def send1(item, slot, sem, who):
        if item < 2:
            src, dst = own1.at[item], u1.at[slot, item]
        else:
            src, dst = bown1.at[item - 2], b1.at[slot, item - 2]
        return remote(src, dst, sem.at[item], sem_1r.at[slot, item], who)

    def to_side1(item):
        return send1(item, side_slot, sem_1z, side)

    def to_mate1(item):
        return send1(item, mate_slot, sem_1m, mate)

    def start1(item):
        if item >= 2:
            when(has_side, lambda: to_side1(item).start())
        to_mate1(item).start()

    def in1(slot, item):
        ref = u1.at[slot - 1, item] if item < 2 else b1.at[slot - 1, item - 2]
        when(has_one[slot], lambda: arrive(ref, sem_1r.at[slot - 1, item]))

    def send2(item, ahead):
        slot = (BW if ahead else FW) - 1
        if item == 0:
            src, dst = own2.at[F if ahead else K], u2.at[slot]
        else:
            src, dst = bown2.at[item - 1], b2.at[slot, item - 1]
        way = 0 if ahead else 1
        return remote(
            src, dst, sem_2s.at[way, item], sem_2r.at[slot, item], fw if ahead else bw
        )

    def start2(item, ahead):
        when(has_fw if ahead else has_bw, lambda: send2(item, ahead).start())

    def in2(slot, item):
        ref = u2.at[slot - 1] if item == 0 else b2.at[slot - 1, item - 1]
        when(has_two[slot], lambda: arrive(ref, sem_2r.at[slot - 1, item]))

    def rhs0(half, *pairs):
        bown1[half] = new_rhs(0, b0[OWN, half], (u0[OWN, K], b0[BW, half]), *pairs)
        start1(2 + half)

    def inner_rhs0(half):
        y_in(8 + half)
        rhs0(half)

    def outer_rhs0(half):
        when(has_bw, lambda: arrive(b0.at[BW, half], sem_d.at[1, half]))
        rhs0(half, (u0[OWN, F], b0[FW, half]))

    def rhs1(half):
        bown2[half] = new_rhs(
            1, bown1[half], (own1[K], b1[BW - 1, half]), (own1[F], b1[FW - 1, half])
        )
        start2(1 + half, True)
        start2(1 + half, False)

    def inverse1():
        inverse((product((own1[K], u1[BW - 1, F]), (own1[F], u1[FW - 1, K])), 1))

    def cross1(unit):
        slot = FW if unit == F else BW
        raw[unit] = crossed(own1[unit], u1[slot - 1, unit])

    @pl.when(inner)
    def _():
        to_mate(K).start()
        to_mate(F).start()
        start_side(BW, SFAR, F)
        wait_rhs()
        for half in range(2):
            to_mate(2 + half).start()
        for item in range(4):
            hand_on(item)
        side_in(SOWN, K)
        side_raw[K] = crossed(u0[SOWN, K], u0[FW, K])
        for item in (4, 5):
            hand_on(item)
        side_in(SOWN, F)
        side_in(SFAR, K)
        inverse((product((u0[SOWN, K], u0[FW, F]), (u0[SOWN, F], u0[SFAR, K])), 3))
        raw[F] = crossed(u0[OWN, F], u0[FW, F])
        u1[FW - 1, K] = solved(3, side_raw[K])
        for item in (6, 7):
            hand_on(item)
        start_side(BW, SFAR, K)
        inverse((product((u0[OWN, K], u0[BW, F]), (u0[OWN, F], u0[FW, K])), 0))
        raw[K] = crossed(u0[OWN, K], u0[BW, K])
        own1[F] = solved(0, raw[F])
        own1[K] = solved(0, raw[K])
        start1(F)
        start1(K)
        side_in(SFAR, F)
        in1(BW, F)
        in1(BW, K)
        inverse1()
        side_raw[F] = crossed(u0[SOWN, F], u0[SFAR, F])
        u1[FW - 1, F] = solved(3, side_raw[F])
        for unit in (F, K):
            cross1(unit)
            own2[unit] = solved(1, raw[unit])
            start2(0, unit == F)
        for half in range(2):
            inner_rhs0(half)
        for half in range(2):
            in1(FW, 2 + half)
            in1(BW, 2 + half)
            rhs1(half)

    @pl.when(outer)
    def _():
        for item in range(4):
            over_y(item).start()
        start_side(OWN, SOWN, K)
        start_side(OWN, SOWN, F)
        mate_in(K)
        for item in (4, 5):
            over_y(item).start()
        start_side(FW, SFAR, K)
        mate_in(F)
        for item in (6, 7):
            over_y(item).start()
        start_side(FW, SFAR, F)
        wait_rhs()
        for half in range(2):
            mate_in(2 + half)
            partial[half] = residual(b0[FW, half], (u0[FW, K], b0[OWN, half]))
        raw[F] = crossed(u0[OWN, F], u0[FW, F])
        side_in(BW, F)
        inverse((product((u0[OWN, K], u0[BW, F]), (u0[OWN, F], u0[FW, K])), 0))
        own1[F] = solved(0, raw[F])
        start1(F)
        side_in(BW, K)
        raw[K] = crossed(u0[OWN, K], u0[BW, K])
        own1[K] = solved(0, raw[K])
        start1(K)
        for item in (6, 7):
            over_y(item).wait_send()
        for half in range(2):
            when(has_bw, lambda half=half: over_diag(half).start())
        when(has_bw, lambda: over_diag(0).wait_send())
        for item in (8, 9):
            over_y(item).start()
        side_in(SOWN, F)
        side_raw[F] = crossed(u0[SOWN, F], u0[BW, F])
        in1(FW, F)
        in1(FW, K)
        cross1(F)
        outer_rhs0(0)
        side_in(SFAR, F)
        side_in(SOWN, K)
        inverse((product((u0[SOWN, K], u0[SFAR, F]), (u0[SOWN, F], u0[BW, K])), 3))
        u1[BW - 1, F] = solved(3, side_raw[F])
        outer_rhs0(1)
        inverse1()
        own2[F] = solved(1, raw[F])
        side_in(SFAR, K)
        side_raw[K] = crossed(u0[SOWN, K], u0[SFAR, K])
        u1[BW - 1, K] = solved(3, side_raw[K])
        cross1(K)
        own2[K] = solved(1, raw[K])
        start2(0, False)
        in1(FW, 2)
        in1(BW, 2)
        rhs1(0)
        start2(0, True)
        in1(FW, 3)
        in1(BW, 3)
        rhs1(1)

    def spot(half, part):
        return (
            last.at[half, :, pl.ds(part * wide, wide)],
            out_ref.at[0, part, :, pl.ds(half * wide, wide)],
        )

    def give(half, part):
        src, dst = spot(half, part)
        return remote(src, dst, sem_out.at[0, half, part], sem_out.at[1, half, part], twin)

    in2(FW, 0)
    in2(BW, 0)
    inverse((product((own2[K], u2[BW - 1]), (own2[F], u2[FW - 1])), 2))
    for half in range(2):
        in2(FW, 1 + half)
        in2(BW, 1 + half)
        rows = new_rhs(
            2, bown2[half], (own2[K], b2[BW - 1, half]), (own2[F], b2[FW - 1, half])
        )

        @pl.when(inner)
        def _():
            last[half] = rows
            for part in range(2):
                give(half, part).start()

        @pl.when(outer)
        def _():
            for part in range(2):
                out_ref[0, part, :, half * wide : (half + 1) * wide] = rows[
                    :, part * wide : (part + 1) * wide
                ]

    @pl.when(inner)
    def _():
        for item in range(4):
            to_mate(item).wait_send()

    @pl.when(outer)
    def _():
        for item in range(10):
            if item not in (6, 7):
                over_y(item).wait_send()
        when(has_bw, lambda: over_diag(1).wait_send())

    def side_sent(source, place):
        for unit in range(2):
            for part in range(2):
                to_side(source, place, unit, part).wait_send()

    @pl.when(inner & has_side)
    def _():
        side_sent(FW, BW)
        side_sent(OWN, SOWN)
        side_sent(BW, SFAR)

    @pl.when(outer & has_side)
    def _():
        side_sent(OWN, SOWN)
        side_sent(FW, SFAR)

    for item in range(4):
        if item >= 2:
            when(has_side, lambda item=item: to_side1(item).wait_send())
        to_mate1(item).wait_send()
    for item in range(3):
        when(has_fw, lambda item=item: send2(item, True).wait_send())
        when(has_bw, lambda item=item: send2(item, False).wait_send())
    for half in range(2):
        for part in range(2):
            when(inner, lambda half=half, part=part: give(half, part).wait())


def local_call(quads, lower, upper, right_side):
    block = lower.shape[1:]
    half = (right_side.shape[2], right_side.shape[3])
    anywhere = pl.BlockSpec(memory_space=pl.ANY)
    dma = pltpu.SemaphoreType.DMA
    vmem = lambda *shape: pltpu.VMEM(shape, LOW)
    return pl.pallas_call(
        functools.partial(kernel, quads),
        out_shape=pltpu.VMEM(right_side.shape, right_side.dtype),
        in_specs=[anywhere] * 3,
        out_specs=pl.BlockSpec(memory_space=pltpu.VMEM),
        scratch_shapes=[
            vmem(5, 2, *block),
            vmem(3, 2, *half),
            vmem(2, *block),
            vmem(2, *half),
            vmem(2, 2, *block),
            vmem(2, 2, *half),
            vmem(2, *block),
            vmem(2, *half),
            vmem(2, *block),
            vmem(2, 2, *half),
            vmem(2, *half),
            vmem(4, *block),
            vmem(2, *block),
            vmem(2, *block),
            vmem(2, *block),
            vmem(2, *block),
            vmem(2, *half),
            dma((2,)),
            dma((2, 2)),
            dma((2, 4)),
            dma((2, 10)),
            dma((2, 2)),
            dma((2, 3, 2, 2)),
            dma((4,)),
            dma((4,)),
            dma((2, 4)),
            dma((2, 3)),
            dma((2, 3)),
            dma((2, 2, 2)),
        ],
        compiler_params=pltpu.CompilerParams(collective_id=0, has_side_effects=True),
    )(lower, upper, right_side)


def solution(mesh):
    placed = P(("energy", "chain"), None, None, None)
    return jax.shard_map(
        functools.partial(local_call, mesh.shape["chain"] // 4),
        mesh=mesh,
        in_specs=(placed,) * 3,
        out_specs=placed,
        check_vma=False,
    )
```

```python
import functools

import jax
import jax.numpy as jnp
from jax import lax
from jax.experimental import pallas as pl
from jax.experimental.pallas import tpu as pltpu
from jax.sharding import PartitionSpec as P

NS_STEPS = 2
MESH = pl.DeviceIdType.MESH
LOW = jnp.bfloat16

F, K = 0, 1
OWN, FW, BW = 0, 1, 2
SOWN, SFAR = 3, 4


def dot(left, right):
    return jnp.dot(left, right, preferred_element_type=jnp.float32)


def product(*pairs):
    left = jnp.concatenate([part for l, _ in pairs for part in (l[0], l[1])], axis=1)
    real = jnp.concatenate([part for _, r in pairs for part in (r[0], -r[1])], axis=0)
    imag = jnp.concatenate([part for _, r in pairs for part in (r[1], r[0])], axis=0)
    return dot(left, real), dot(left, imag)


def rhs_product(*pairs):
    left = jnp.concatenate([part for l, _ in pairs for part in (l[0], l[1])], axis=1)
    right = []
    for _, r in pairs:
        wide = r.shape[1] // 2
        right += [r, jnp.concatenate([-r[:, wide:], r[:, :wide]], axis=1)]
    return dot(left, jnp.concatenate(right, axis=0))


def rounded(parts):
    return jnp.stack([parts[0].astype(LOW), parts[1].astype(LOW)])


def negated(parts):
    return -parts[0], -parts[1]


def kernel(
    quads, l_ref, u_ref, b_ref, out_ref,
    u0, b0, own1, bown1, u1, b1, own2, bown2, u2, b2, last, inv, raw, side_raw, low, fix, partial,
    sem_load, sem_bload, sem_m, sem_y, sem_d, sem_s,
    sem_1m, sem_1z, sem_1r, sem_2s, sem_2r, sem_out,
):
    me = lax.axis_index("chain")
    q = me // 4
    a = (me // 2) % 2
    b = me % 2
    inner = a != b
    outer = a == b
    qf, qb = q + 1 - 2 * a, q - 1 + 2 * a
    has_fw = (qf >= 0) & (qf < quads)
    has_bw = (qb >= 0) & (qb < quads)
    order = l_ref.shape[2]
    wide = b_ref.shape[3] // 2

    def at(quad, y, core):
        return {"chain": quad * 4 + y * 2 + core}

    mate = at(q, a, 1 - b)
    across = at(q, 1 - a, b)
    twin = at(q, b, a)
    fw, bw = at(qf, a, b), at(qb, a, b)
    side = {"chain": jnp.where(inner, at(qf, a, 1 - b)["chain"], at(qb, a, 1 - b)["chain"])}
    has_side = (inner & has_fw) | (outer & has_bw)
    diag = at(qb, 1 - a, 1 - b)
    has_diag = outer & has_bw

    def local(src, dst, sem):
        return pltpu.make_async_copy(src, dst, sem)

    def remote(src, dst, send, recv, who):
        return pltpu.make_async_remote_copy(
            src_ref=src, dst_ref=dst, send_sem=send, recv_sem=recv,
            device_id=who, device_id_type=MESH,
        )

    def arrive(ref, sem):
        pltpu.make_async_copy(ref, ref, sem).wait()

    def when(condition, action):
        pl.when(condition)(action)

    home = jnp.where(outer, OWN, BW)

    def load(unit):
        place = jnp.where(a == 0, 1 - unit, unit)
        return local((l_ref, u_ref)[unit].at[0], u0.at[home, place], sem_load.at[unit])

    def load_rhs(half, part):
        return local(
            b_ref.at[0, part, :, pl.ds(half * wide, wide)],
            b0.at[home, half, :, pl.ds(part * wide, wide)],
            sem_bload.at[half, part],
        )

    barrier = pltpu.get_barrier_semaphore()

    def greet(who):
        pl.semaphore_signal(barrier, inc=1, device_id=who, device_id_type=MESH)

    greet(mate)
    greet(across)
    greetings = ((has_side, side), (has_diag, diag), (inner, twin), (has_fw, fw), (has_bw, bw))
    count = 2
    for exists, who in greetings:
        when(exists, functools.partial(greet, who))
        count = count + exists.astype(jnp.int32)

    for unit in range(2):
        load(unit).start()
    for half in range(2):
        for part in range(2):
            load_rhs(half, part).start()

    def clear(ref):
        ref[...] = jnp.zeros(ref.shape, ref.dtype)

    has_one = {FW: outer | has_fw, BW: inner | has_bw}
    has_two = {FW: has_fw, BW: has_bw}

    @pl.when(outer & jnp.logical_not(has_bw))
    def _():
        clear(u0.at[BW])
        clear(b0.at[BW])

    @pl.when(jnp.logical_not(has_side))
    def _():
        clear(u0.at[SOWN])
        clear(u0.at[SFAR])

    for slot in (FW, BW):
        @pl.when(jnp.logical_not(has_one[slot]))
        def _():
            clear(b1.at[slot - 1])

        @pl.when(jnp.logical_not(has_two[slot]))
        def _():
            clear(u2.at[slot - 1])
            clear(b2.at[slot - 1])

    for unit in range(2):
        load(unit).wait()
    pl.semaphore_wait(barrier, count)

    def to_mate(item):
        if item < 2:
            src, dst = u0.at[BW, item], u0.at[FW, item]
        else:
            src, dst = b0.at[BW, item - 2], b0.at[FW, item - 2]
        return remote(src, dst, sem_m.at[0, item], sem_m.at[1, item], mate)

    def mate_in(item):
        ref = u0.at[FW, item] if item < 2 else b0.at[FW, item - 2]
        arrive(ref, sem_m.at[1, item])

    def y_place(item):
        if item < 8:
            return u0.at[FW if item < 4 else OWN, (item // 2) % 2, item % 2]
        return b0.at[OWN, item % 2]

    def over_y(item):
        if item < 8:
            src = u0.at[OWN if item < 4 else FW, 1 - (item // 2) % 2, item % 2]
        else:
            src = partial.at[item % 2]
        return remote(src, y_place(item), sem_y.at[0, item], sem_y.at[1, item], across)

    def y_in(item):
        arrive(y_place(item), sem_y.at[1, item])

    def to_side(source, place, unit, part):
        return remote(
            u0.at[source, unit, part], u0.at[place, unit, part],
            sem_s.at[0, place - BW, unit, part], sem_s.at[1, place - BW, unit, part], side,
        )

    def start_side(source, place, unit):
        for part in range(2):
            when(has_side, lambda part=part: to_side(source, place, unit, part).start())

    def side_in(place, unit):
        for part in range(2):
            ref, sem = u0.at[place, unit, part], sem_s.at[1, place - BW, unit, part]
            when(has_side, lambda ref=ref, sem=sem: arrive(ref, sem))

    def hand_on(item):
        y_in(item)
        source, place = (FW, BW) if item < 4 else (OWN, SOWN)
        when(has_side, lambda: to_side(source, place, (item // 2) % 2, item % 2).start())

    def over_diag(half):
        return remote(
            b0.at[OWN, half], b0.at[BW, half], sem_d.at[0, half], sem_d.at[1, half], diag
        )

    def wait_rhs():
        for half in range(2):
            for part in range(2):
                load_rhs(half, part).wait()

    row = lax.broadcasted_iota(jnp.int32, (order, order), 0)
    col = lax.broadcasted_iota(jnp.int32, (order, order), 1)
    unit_matrix = (row == col).astype(jnp.float32)

    def inverse(*jobs):
        for place, (off, number) in enumerate(jobs):
            low[place] = rounded((unit_matrix - off[0], -off[1]))
            inv[number] = rounded((unit_matrix + off[0], off[1]))
        for _ in range(NS_STEPS):
            for place, (_, number) in enumerate(jobs):
                prod = product((low[place], inv[number]))
                fix[place] = rounded((2.0 * unit_matrix - prod[0], -prod[1]))
            for place, (_, number) in enumerate(jobs):
                inv[number] = rounded(product((inv[number], fix[place])))

    def crossed(left, right):
        return rounded(negated(product((left, right))))

    def solved(number, right):
        return rounded(product((inv[number], right)))

    def residual(own, *pairs):
        return (own.astype(jnp.float32) - rhs_product(*pairs)).astype(LOW)

    def new_rhs(number, own, *pairs):
        return rhs_product((inv[number], residual(own, *pairs))).astype(LOW)

    mate_slot = jnp.where(outer, BW - 1, FW - 1)
    side_slot = jnp.where(outer, FW - 1, BW - 1)

    def send1(item, slot, sem, who):
        if item < 2:
            src, dst = own1.at[item], u1.at[slot, item]
        else:
            src, dst = bown1.at[item - 2], b1.at[slot, item - 2]
        return remote(src, dst, sem.at[item], sem_1r.at[slot, item], who)

    def to_side1(item):
        return send1(item, side_slot, sem_1z, side)

    def to_mate1(item):
        return send1(item, mate_slot, sem_1m, mate)

    def start1(item):
        if item >= 2:
            when(has_side, lambda: to_side1(item).start())
        to_mate1(item).start()

    def in1(slot, item):
        ref = u1.at[slot - 1, item] if item < 2 else b1.at[slot - 1, item - 2]
        when(has_one[slot], lambda: arrive(ref, sem_1r.at[slot - 1, item]))

    def send2(item, ahead):
        slot = (BW if ahead else FW) - 1
        if item == 0:
            src, dst = own2.at[F if ahead else K], u2.at[slot]
        else:
            src, dst = bown2.at[item - 1], b2.at[slot, item - 1]
        way = 0 if ahead else 1
        return remote(
            src, dst, sem_2s.at[way, item], sem_2r.at[slot, item], fw if ahead else bw
        )

    def start2(item, ahead):
        when(has_fw if ahead else has_bw, lambda: send2(item, ahead).start())

    def in2(slot, item):
        ref = u2.at[slot - 1] if item == 0 else b2.at[slot - 1, item - 1]
        when(has_two[slot], lambda: arrive(ref, sem_2r.at[slot - 1, item]))

    def rhs0(half, *pairs):
        bown1[half] = new_rhs(0, b0[OWN, half], (u0[OWN, K], b0[BW, half]), *pairs)
        start1(2 + half)

    def inner_rhs0(half):
        y_in(8 + half)
        rhs0(half)

    def outer_rhs0(half):
        when(has_bw, lambda: arrive(b0.at[BW, half], sem_d.at[1, half]))
        rhs0(half, (u0[OWN, F], b0[FW, half]))

    def rhs1(half):
        bown2[half] = new_rhs(
            1, bown1[half], (own1[K], b1[BW - 1, half]), (own1[F], b1[FW - 1, half])
        )
        start2(1 + half, True)
        start2(1 + half, False)

    def inverse1():
        inverse((product((own1[K], u1[BW - 1, F]), (own1[F], u1[FW - 1, K])), 1))

    def cross1(unit):
        slot = FW if unit == F else BW
        raw[unit] = crossed(own1[unit], u1[slot - 1, unit])

    @pl.when(inner)
    def _():
        to_mate(K).start()
        to_mate(F).start()
        start_side(BW, SFAR, F)
        wait_rhs()
        for half in range(2):
            to_mate(2 + half).start()
        for item in range(4):
            hand_on(item)
        side_in(SOWN, K)
        side_raw[K] = crossed(u0[SOWN, K], u0[FW, K])
        for item in (4, 5):
            hand_on(item)
        side_in(SOWN, F)
        side_in(SFAR, K)
        inverse((product((u0[SOWN, K], u0[FW, F]), (u0[SOWN, F], u0[SFAR, K])), 3))
        raw[F] = crossed(u0[OWN, F], u0[FW, F])
        u1[FW - 1, K] = solved(3, side_raw[K])
        for item in (6, 7):
            hand_on(item)
        start_side(BW, SFAR, K)
        inverse((product((u0[OWN, K], u0[BW, F]), (u0[OWN, F], u0[FW, K])), 0))
        raw[K] = crossed(u0[OWN, K], u0[BW, K])
        own1[F] = solved(0, raw[F])
        own1[K] = solved(0, raw[K])
        start1(F)
        start1(K)
        side_in(SFAR, F)
        in1(BW, F)
        in1(BW, K)
        inverse1()
        side_raw[F] = crossed(u0[SOWN, F], u0[SFAR, F])
        u1[FW - 1, F] = solved(3, side_raw[F])
        for unit in (F, K):
            cross1(unit)
            own2[unit] = solved(1, raw[unit])
            start2(0, unit == F)
        for half in range(2):
            inner_rhs0(half)
        for half in range(2):
            in1(FW, 2 + half)
            in1(BW, 2 + half)
            rhs1(half)

    @pl.when(outer)
    def _():
        for item in range(4):
            over_y(item).start()
        start_side(OWN, SOWN, K)
        start_side(OWN, SOWN, F)
        mate_in(K)
        for item in (4, 5):
            over_y(item).start()
        start_side(FW, SFAR, K)
        mate_in(F)
        for item in (6, 7):
            over_y(item).start()
        start_side(FW, SFAR, F)
        wait_rhs()
        for half in range(2):
            mate_in(2 + half)
            partial[half] = residual(b0[FW, half], (u0[FW, K], b0[OWN, half]))
        raw[F] = crossed(u0[OWN, F], u0[FW, F])
        side_in(BW, F)
        inverse((product((u0[OWN, K], u0[BW, F]), (u0[OWN, F], u0[FW, K])), 0))
        own1[F] = solved(0, raw[F])
        start1(F)
        side_in(BW, K)
        raw[K] = crossed(u0[OWN, K], u0[BW, K])
        own1[K] = solved(0, raw[K])
        start1(K)
        for item in (6, 7):
            over_y(item).wait_send()
        for half in range(2):
            when(has_bw, lambda half=half: over_diag(half).start())
        when(has_bw, lambda: over_diag(0).wait_send())
        for item in (8, 9):
            over_y(item).start()
        side_in(SOWN, F)
        side_raw[F] = crossed(u0[SOWN, F], u0[BW, F])
        in1(FW, F)
        in1(FW, K)
        cross1(F)
        outer_rhs0(0)
        side_in(SFAR, F)
        side_in(SOWN, K)
        inverse((product((u0[SOWN, K], u0[SFAR, F]), (u0[SOWN, F], u0[BW, K])), 3))
        u1[BW - 1, F] = solved(3, side_raw[F])
        outer_rhs0(1)
        inverse1()
        own2[F] = solved(1, raw[F])
        side_in(SFAR, K)
        side_raw[K] = crossed(u0[SOWN, K], u0[SFAR, K])
        u1[BW - 1, K] = solved(3, side_raw[K])
        cross1(K)
        own2[K] = solved(1, raw[K])
        start2(0, False)
        in1(FW, 2)
        in1(BW, 2)
        rhs1(0)
        start2(0, True)
        in1(FW, 3)
        in1(BW, 3)
        rhs1(1)

    def spot(half, part):
        return (
            last.at[half, :, pl.ds(part * wide, wide)],
            out_ref.at[0, part, :, pl.ds(half * wide, wide)],
        )

    def give(half, part):
        src, dst = spot(half, part)
        return remote(src, dst, sem_out.at[0, half, part], sem_out.at[1, half, part], twin)

    in2(FW, 0)
    in2(BW, 0)
    inverse((product((own2[K], u2[BW - 1]), (own2[F], u2[FW - 1])), 2))
    for half in range(2):
        in2(FW, 1 + half)
        in2(BW, 1 + half)
        rows = new_rhs(
            2, bown2[half], (own2[K], b2[BW - 1, half]), (own2[F], b2[FW - 1, half])
        )

        @pl.when(inner)
        def _():
            last[half] = rows
            for part in range(2):
                give(half, part).start()

        @pl.when(outer)
        def _():
            for part in range(2):
                out_ref[0, part, :, half * wide : (half + 1) * wide] = rows[
                    :, part * wide : (part + 1) * wide
                ]

    @pl.when(inner)
    def _():
        for item in range(4):
            to_mate(item).wait_send()

    @pl.when(outer)
    def _():
        for item in range(10):
            if item not in (6, 7):
                over_y(item).wait_send()
        when(has_bw, lambda: over_diag(1).wait_send())

    def side_sent(source, place):
        for unit in range(2):
            for part in range(2):
                to_side(source, place, unit, part).wait_send()

    @pl.when(inner & has_side)
    def _():
        side_sent(FW, BW)
        side_sent(OWN, SOWN)
        side_sent(BW, SFAR)

    @pl.when(outer & has_side)
    def _():
        side_sent(OWN, SOWN)
        side_sent(FW, SFAR)

    for item in range(4):
        if item >= 2:
            when(has_side, lambda item=item: to_side1(item).wait_send())
        to_mate1(item).wait_send()
    for item in range(3):
        when(has_fw, lambda item=item: send2(item, True).wait_send())
        when(has_bw, lambda item=item: send2(item, False).wait_send())
    for half in range(2):
        for part in range(2):
            when(inner, lambda half=half, part=part: give(half, part).wait())


def local_call(quads, lower, upper, right_side):
    block = lower.shape[1:]
    half = (right_side.shape[2], right_side.shape[3])
    anywhere = pl.BlockSpec(memory_space=pl.ANY)
    dma = pltpu.SemaphoreType.DMA
    vmem = lambda *shape: pltpu.VMEM(shape, LOW)
    return pl.pallas_call(
        functools.partial(kernel, quads),
        out_shape=pltpu.VMEM(right_side.shape, right_side.dtype),
        in_specs=[anywhere] * 3,
        out_specs=pl.BlockSpec(memory_space=pltpu.VMEM),
        scratch_shapes=[
            vmem(5, 2, *block),
            vmem(3, 2, *half),
            vmem(2, *block),
            vmem(2, *half),
            vmem(2, 2, *block),
            vmem(2, 2, *half),
            vmem(2, *block),
            vmem(2, *half),
            vmem(2, *block),
            vmem(2, 2, *half),
            vmem(2, *half),
            vmem(4, *block),
            vmem(2, *block),
            vmem(2, *block),
            vmem(2, *block),
            vmem(2, *block),
            vmem(2, *half),
            dma((2,)),
            dma((2, 2)),
            dma((2, 4)),
            dma((2, 10)),
            dma((2, 2)),
            dma((2, 3, 2, 2)),
            dma((4,)),
            dma((4,)),
            dma((2, 4)),
            dma((2, 3)),
            dma((2, 3)),
            dma((2, 2, 2)),
        ],
        compiler_params=pltpu.CompilerParams(collective_id=0, has_side_effects=True),
    )(lower, upper, right_side)


def solution(mesh):
    placed = P(("energy", "chain"), None, None, None)
    return jax.shard_map(
        functools.partial(local_call, mesh.shape["chain"] // 4),
        mesh=mesh,
        in_specs=(placed,) * 3,
        out_specs=placed,
        check_vma=False,
    )
```
